512 devices in a mesh: row: 32 (over z, y_hi), col: 16 (over y_lo, x, core).
Axes of the slice: x: 4, y: 8 (y_hi: 4, y_lo: 2; y = y_hi * 2 + y_lo), z: 8, core: 2. Of those that a mesh axis runs over, the one named last changes fastest.
Arguments:
- panel_xyz: float32 [3, 65536], P(None, ('col', 'row')), may hold values from -1.2 to 1.2, as said below
- panel_weight: float32 [1, 65536], P(None, ('col', 'row')), may hold values from 0.3 to 3
- self_term: float32 [65536], P(('col', 'row')), may hold values from 2 to 6
- panel_slot: int32 [65536], P(('col', 'row')), may hold values from 0 to 127, as said below
- block_inverse: float32 [64, 65536], P(None, ('col', 'row')), may hold values from -0.75 to 0.75
- incident: float32 [16, 65536], P(None, ('col', 'row')), may hold values from -6 to 6
- field_xyz: float32 [3, 16384], P(None, 'row'), may hold values from -2.5 to 2.5
- field_group: int32 [16384], P(('row', 'col')), may hold values from 0 to 127
Outputs:
- density: float32 [16, 65536], P(None, ('col', 'row'))
- potential: bfloat16 [16, 16384], P(None, ('row', 'col'))
- detector: float32 [16, 128], replicated
The draws below stay inside these ranges and needn't reach their ends.
Inputs may be any that keep to these rules, and one draw needn't show every extreme that they name: Within each aligned run of 128 panels, panel_slot is a permutation of 0 to 127. `panel_xyz`: panel centres lie on a closed surface around the anchor.
All inputs are finite; a program needn't handle non-finite values.
Results may differ from the reference program's by a relative error of at most 0.018.
Values may be sent and summed in bfloat16 or wider, within the bound.
A program may use at most 64 MiB of HBM per device.

```python
import math
import jax
import jax.numpy as jnp
from jax import lax

SHARD = 128
WAVES = 16
BS = 64
GROUPS = 128
N = 65536
FIELDS = 16384


def draw_panel_xyz(key, part):
    vectors = jax.random.normal(key, (3, N), jnp.float32)
    vectors = vectors / jnp.sqrt(jnp.sum(vectors * vectors, axis=0, keepdims=True) + 1e-12)
    return vectors


def draw_panel_slot(key, part):
    subkeys = jax.random.split(jax.random.fold_in(key, 17), N // SHARD)
    orders = jax.vmap(lambda subkey: jax.random.permutation(subkey, SHARD))(subkeys)
    return orders.reshape(N).astype(jnp.int32)


def with_ends(values, own_key, least, top_value):
    index_at = [jax.random.randint(jax.random.fold_in(own_key, axis), (), 0, length) for axis, length in enumerate(values.shape)]
    longest = values.shape.index(max(values.shape))
    beside = index_at[:longest] + [(index_at[longest] + 1) % values.shape[longest]] + index_at[longest + 1:]
    return values.at[tuple(index_at)].set(least).at[tuple(beside)].set(top_value)


def block_levels(own_key, dims, cuts, least, high):
    def one(dim, parts):
        steps = jax.random.uniform(jax.random.fold_in(jax.random.fold_in(own_key, 6), dim), (parts,), jnp.float32, least / len(cuts), high / len(cuts))
        return jnp.repeat(jnp.exp(steps), dims[dim] // parts).reshape((-1,) + (1,) * (len(dims) - dim - 1))

    level = one(*cuts[0])
    for cut in cuts[1:]:
        level = level * one(*cut)
    return level


def bell_draw(own_key, extent, deviation, most, cuts=(), kind=jnp.bfloat16):
    drawn = deviation * jax.random.normal(own_key, extent, jnp.float32)
    if cuts:
        drawn = drawn * block_levels(own_key, extent, cuts, -0.22, 0.18)
    return jnp.clip(drawn, -most, most).astype(kind)


def setup_inputs(seed: int = 0) -> dict:
    key_of = jax.random.split(jax.random.key(seed), 9)
    return {
        "panel_xyz": draw_panel_xyz(jax.random.fold_in(key_of[8], 71), 0),
        "panel_weight": jnp.clip(jnp.exp(math.log(3.0) - 2.3025851 * jax.random.uniform(key_of[1], (1, N), jnp.float32) ** block_levels(key_of[1], (1, N), ((1, 512),), -0.2, 0.2)), 0.3, 3.0),
        "self_term": jnp.clip(jnp.exp(math.log(6.0) - 1.0986123 * jax.random.uniform(key_of[2], (N,), jnp.float32) ** block_levels(key_of[2], (N,), ((0, 512),), -0.2, 0.2)), 2.0, 6.0),
        "panel_slot": draw_panel_slot(jax.random.fold_in(key_of[8], 71), 0),
        "block_inverse": bell_draw(key_of[4], (BS, N), BS ** -0.5, 0.75, ((1, 512),), jnp.float32),
        "incident": bell_draw(key_of[5], (WAVES, N), 1.0, 6.0, ((1, 512),), jnp.float32),
        "field_xyz": jnp.clip(jax.random.uniform(key_of[6], (3, FIELDS), jnp.float32, -2.5, 2.5) * block_levels(key_of[6], (3, FIELDS), ((1, 32),), -0.4, 0.0), -2.5, 2.5),
        "field_group": with_ends(jax.random.randint(key_of[7], (FIELDS,), 0, GROUPS), jax.random.fold_in(key_of[7], 1), 0, GROUPS - 1).astype(jnp.int32),
    }


wave_number = 12.0
smoothing = 0.05
damping = 0.5

def kernel_tile(targets, sources, source_weight, coupling):
    delta_x = targets[0][:, None] - sources[0][None, :]
    delta_y = targets[1][:, None] - sources[1][None, :]
    delta_z = targets[2][:, None] - sources[2][None, :]
    dist_sq = delta_x * delta_x + delta_y * delta_y + delta_z * delta_z
    radius = jnp.sqrt(dist_sq)
    entries = coupling * source_weight[None, :] * jnp.cos(wave_number * radius) * lax.rsqrt(dist_sq + smoothing * smoothing)
    return entries.astype(jnp.bfloat16)

def local_precondition(residual, panel_slot, block_inverse, self_term):
    block_size = block_inverse.shape[0]
    position = panel_slot % block_size
    block_of = panel_slot // block_size
    selector = (position[:, None] == jnp.arange(block_size, dtype=jnp.int32)[None, :]).astype(jnp.float32)
    chosen = jnp.dot(selector, block_inverse, precision=lax.Precision.HIGHEST, preferred_element_type=jnp.float32)
    coupled = jnp.where(block_of[:, None] == block_of[None, :], chosen, jnp.zeros_like(chosen))
    mixing = lax.dot_general(residual, coupled, (((1,), (1,)), ((), ())), precision=lax.Precision.HIGHEST, preferred_element_type=jnp.float32)
    return residual / self_term[None, :] + mixing

def reference(panel_xyz, panel_weight, self_term, panel_slot, block_inverse, incident, field_xyz, field_group):
    run_count = N // SHARD
    coupling = 1.0 / math.sqrt(N)
    weights = panel_weight[0]

    def precondition(values):
        spread = values.reshape(WAVES, run_count, SHARD).transpose(1, 0, 2)
        slots = panel_slot.reshape(run_count, SHARD)
        inverses = block_inverse.reshape(BS, run_count, SHARD).transpose(1, 0, 2)
        selfs = self_term.reshape(run_count, SHARD)
        result = jax.vmap(local_precondition)(spread, slots, inverses, selfs)
        return result.transpose(1, 0, 2).reshape(WAVES, N)

    def apply_kernel(targets_all, count, densities):
        block_rows = math.gcd(count, 512)
        blocks = targets_all.reshape(3, count // block_rows, block_rows).transpose(1, 0, 2)

        def one_block(targets):
            kernel = kernel_tile(targets, panel_xyz, weights, coupling)
            return lax.dot_general(densities, kernel, (((1,), (1,)), ((), ())), preferred_element_type=jnp.float32)
        result = lax.map(one_block, blocks)
        return result.transpose(1, 0, 2).reshape(WAVES, count)
    start = precondition(incident)
    start_b = start.astype(jnp.bfloat16)
    images = apply_kernel(panel_xyz, N, start_b)
    residual = incident - self_term[None, :] * start - images
    density = start + damping * precondition(residual)
    density_b = density.astype(jnp.bfloat16)
    field_sum = apply_kernel(field_xyz, FIELDS, density_b)
    onehot = (field_group[:, None] == jnp.arange(GROUPS, dtype=jnp.int32)[None, :]).astype(jnp.float32)
    group_sums = jnp.dot(field_sum, onehot, precision=lax.Precision.HIGHEST, preferred_element_type=jnp.float32)
    detector = group_sums / math.sqrt(FIELDS / GROUPS)
    return (density, field_sum.astype(jnp.bfloat16), detector)
```

```python
import functools
import math

import jax
import jax.numpy as jnp
import numpy as np
from jax import lax
from jax.experimental import pallas as pl
from jax.experimental.pallas import tpu as pltpu
from jax.sharding import PartitionSpec as P

MESH = pl.DeviceIdType.MESH
HIGHEST = lax.Precision.HIGHEST
F32 = jnp.float32
BF16 = jnp.bfloat16

GROUPS = 128
SH = 128
WV = 16
FD = 32
wave_number = 12.0
smoothing = 0.05
damping = 0.5

B0, B1, B2, B3 = 6.283164041181243, -41.33714186520903, 81.3407492682057, -70.99322232997507
CYCLES = wave_number / (2.0 * math.pi)
EPS = smoothing * smoothing * CYCLES * CYCLES


def selectors():
    sel_b = np.zeros((16, 32), np.float32)
    sel_a = np.zeros((32, 16), np.float32)
    high, mid, low = 0, 1, 2
    pairs = [(high, high), (high, mid), (mid, high), (mid, mid), (high, low), (low, high), (mid, low), (low, mid)]
    k = 0
    for b, a in pairs:
        for c in range(3):
            sel_b[3 * b + c, k] = -2.0
            sel_a[k, 3 * a + c] = 1.0
            k += 1
    for n in range(3):
        sel_b[9 + n, k] = 1.0
        sel_a[k, 12] = 1.0
        k += 1
    for n in range(3):
        sel_b[12, k] = 1.0
        sel_a[k, 9 + n] = 1.0
        k += 1
    return sel_b, sel_a


def split3(x):
    h = x.astype(BF16).astype(F32)
    m = (x - h).astype(BF16).astype(F32)
    return h, m, (x - h) - m


def geometry(scr, xyz):
    c = xyz * CYCLES
    h, m, l = split3(c)
    nh, nm, nl = split3(jnp.sum(c * c, axis=0, keepdims=True))
    scr[0:3, :] = h
    scr[3:6, :] = m
    scr[6:9, :] = l
    scr[9:10, :] = nh
    scr[10:11, :] = nm
    scr[11:12, :] = nl
    scr[12:13, :] = jnp.ones_like(nh)
    scr[13:16, :] = jnp.zeros((3, c.shape[1]), F32)
    return scr[...].astype(BF16)


def pair_values(d):
    s = jnp.maximum(d, 1e-12)
    r = s * lax.rsqrt(s)
    v = 0.25 - jnp.abs(r - jnp.round(r))
    q = v * v
    p = ((q + B2 / B3) * q + B1 / B3) * q + B0 / B3
    return ((p * v) * lax.rsqrt(s + EPS)).astype(BF16)


def kernel(
    nz, ny, nc, scale, wave_scale,
    xyz, weight, self_term, slot, binv, inc, fxyz, fgroup, sel_b, sel_a,
    den_o, pot_o, det_o,
    geo_s, fgeo_s, fg_s, src, tgt, feat_a, feat_f, coupled, acc, rs_out, rs_in, den, gf, facc,
    pot_out, pot_in, fgs, det1, det2,
    src_ss, src_rs, tgt_ss, tgt_rs, rs_ss, rs_rs, den_ss, den_rs, pot_ss, pot_rs, fg_ss, fg_rs,
    d1_ss, d1_rs, d2_ss, d2_rs,
):
    nr = nz * ny
    fb = facc.shape[1] // 128
    i = lax.axis_index("row")
    j = lax.axis_index("col")
    iz, iy = i // ny, i % ny

    def hops(d):
        dz, dy = d
        return min(dz, nz - dz) + 2 * min(dy, ny - dy)

    offsets = sorted(((dz, dy) for dz in range(nz) for dy in range(ny)), key=hops)

    barrier = pltpu.get_barrier_semaphore()

    def greet_row(n, _):
        pl.semaphore_signal(barrier, inc=1, device_id=(lax.rem(i + n, nr), j), device_id_type=MESH)
        return 0

    def greet_col(n, _):
        pl.semaphore_signal(barrier, inc=1, device_id=(i, lax.rem(j + n, nc)), device_id_type=MESH)
        return 0

    lax.fori_loop(1, nr, greet_row, 0)
    lax.fori_loop(1, nc, greet_col, 0)

    packet = geometry(geo_s, xyz[...])
    src[0, 0:16, :] = packet
    tgt[0] = packet
    place = lax.broadcasted_iota(jnp.int32, (64, SH), 0)
    chosen = (place == slot[...] % 64).astype(F32)
    half = (lax.broadcasted_iota(jnp.int32, (8, SH), 0) == slot[...] // 64).astype(F32)
    over_rows = (((0,), (0,)), ((), ()))
    picked = lax.dot_general(binv[...], chosen, over_rows, precision=HIGHEST, preferred_element_type=F32)
    same = lax.dot_general(half, half, over_rows, preferred_element_type=F32)
    coupled[...] = picked * same

    def precondition(values):
        mixing = jnp.dot(values, coupled[...], precision=HIGHEST, preferred_element_type=F32)
        return values / self_term[...] + mixing

    start = precondition(inc[...])
    src[0, 16:32, :] = (start * weight[...]).astype(BF16)
    fg_s[...] = jnp.zeros_like(fg_s)
    fg_s[:, 0:FD] = jnp.broadcast_to(fgroup[...].astype(F32), (8, FD))
    fgs[j] = fg_s[...]

    pl.semaphore_wait(barrier, nr + nc - 2)

    def row_copy(k, src_ref, dst_ref, ss, rs):
        dz, dy = offsets[k]
        peer = lax.rem(iz + (nz - dz), nz) * ny + lax.rem(iy + (ny - dy), ny)
        return pltpu.make_async_remote_copy(
            src_ref=src_ref, dst_ref=dst_ref, send_sem=ss.at[k], recv_sem=rs.at[k],
            device_id=(peer, j), device_id_type=MESH,
        )

    def col_copy(k, src_ref, dst_ref, ss, rs, sem):
        return pltpu.make_async_remote_copy(
            src_ref=src_ref, dst_ref=dst_ref, send_sem=ss.at[k], recv_sem=rs.at[sem],
            device_id=(i, lax.rem(j + k, nc)), device_id_type=MESH,
        )

    def each(lo, hi, body):
        def step(n, _):
            body(n)
            return 0

        lax.fori_loop(lo, hi, step, 0)

    each(1, nc, lambda k: col_copy(k, tgt.at[0], tgt.at[k], tgt_ss, tgt_rs, k).start())
    for k in range(nr - 1, 0, -1):
        row_copy(k, src.at[0], src.at[k], src_ss, src_rs).start()
    each(1, nc, lambda k: col_copy(k, fgs.at[j], fgs.at[j], fg_ss, fg_rs, k).start())

    def features_a(pk):
        return jnp.dot(sel_a[...], pk, preferred_element_type=F32).astype(BF16)

    def features_b(pk):
        return lax.dot_general(pk, sel_b[...], over_rows, preferred_element_type=F32).astype(BF16)

    feat_f[...] = features_a(geometry(fgeo_s, fxyz[...]))
    acc[...] = jnp.zeros_like(acc)

    def tgt_wait(k):
        col_copy(0, tgt.at[0], tgt.at[k], tgt_ss, tgt_rs, k).wait_recv()
        feat_a[:, pl.ds(pl.multiple_of(k * SH, SH), SH)] = features_a(tgt[k])

    feat_a[:, 0:SH] = features_a(tgt[0])
    each(1, nc, tgt_wait)

    def plain_wait(k, buf, rs):
        pltpu.make_async_remote_copy(
            src_ref=buf.at[0], dst_ref=buf.at[0], send_sem=rs.at[k], recv_sem=rs.at[k],
            device_id=(i, j), device_id_type=MESH,
        ).wait_recv()

    tb = min(1024, nc * SH)

    def images_chunk(c):
        @pl.when(c > 0)
        def _():
            plain_wait(2 * c, src, src_rs)

        plain_wait(2 * c + 1, src, src_rs)
        one, two = src[2 * c], src[2 * c + 1]
        b = features_b(jnp.concatenate([one[0:16], two[0:16]], axis=1))
        x = jnp.concatenate([one[16:32], two[16:32]], axis=1)

        def tile(t):
            cols = pl.ds(pl.multiple_of(t * tb, tb), tb)
            g = pair_values(jnp.dot(b, feat_a[:, cols], preferred_element_type=F32))
            acc[:, cols] += jnp.dot(x, g, preferred_element_type=F32)

        each(0, nc * SH // tb, tile)

    each(0, nr // 2, images_chunk)

    def rs_send(k):
        rs_out[k] = acc[:, pl.ds(pl.multiple_of(k * SH, SH), SH)].astype(BF16)
        back = lax.rem(nc - k, nc)
        pltpu.make_async_remote_copy(
            src_ref=rs_out.at[k], dst_ref=rs_in.at[k], send_sem=rs_ss.at[k], recv_sem=rs_rs.at[k],
            device_id=(i, lax.rem(j + back, nc)), device_id_type=MESH,
        ).start()

    each(1, nc, rs_send)

    def field_chunk(c):
        one, two = src[2 * c], src[2 * c + 1]
        b = features_b(jnp.concatenate([one[0:16], two[0:16]], axis=1))
        gf[c] = pair_values(jnp.dot(b, feat_f[...], preferred_element_type=F32))

    early = nr // 2 * 3 // 8
    each(0, early, field_chunk)

    rs_in[0] = jnp.zeros((WV, SH), BF16)
    each(1, nc, lambda k: plain_wait(k, rs_in, rs_rs))
    total = acc[:, 0:SH] + jnp.sum(rs_in[...].astype(F32), axis=0)
    residual = inc[...] - self_term[...] * start - total * scale
    density = start + damping * precondition(residual)
    den_o[...] = density
    den[0] = (density * weight[...]).astype(BF16)
    for k in range(nr - 1, 0, -1):
        row_copy(k, den.at[0], den.at[k], den_ss, den_rs).start()

    each(early, nr // 2, field_chunk)
    facc[...] = jnp.zeros_like(facc)

    def field_sum(c):
        @pl.when(c > 0)
        def _():
            plain_wait(2 * c, den, den_rs)

        plain_wait(2 * c + 1, den, den_rs)
        x = jnp.concatenate([den[2 * c], den[2 * c + 1]], axis=1)
        facc[...] += jnp.dot(x, gf[c], preferred_element_type=F32)

    each(0, nr // 2, field_sum)

    facc[...] = facc[...] * scale
    for b in range(fb):
        pot_out[b] = facc[:, b * 128:(b + 1) * 128].astype(BF16)

    each(1, nc, lambda k: col_copy(k, fgs.at[j], fgs.at[j], fg_ss, fg_rs, k).wait_recv())
    each(1, nc, lambda k: col_copy(k, pot_out.at[lax.rem(j + k, nc) // 4], pot_in.at[k], pot_ss, pot_rs, k).start())

    part = jnp.zeros((WV, GROUPS), F32)
    detectors = lax.broadcasted_iota(jnp.int32, (GROUPS, 128), 0).astype(F32)
    for b in range(fb):
        groups = fgs[4 * b]
        for m in range(1, 4):
            groups = groups + pltpu.roll(fgs[4 * b + m], FD * m, 1)
        onehot = (detectors == groups[0:1, :]).astype(F32)
        part = part + lax.dot_general(
            facc[:, b * 128:(b + 1) * 128], onehot, (((1,), (1,)), ((), ())), precision=HIGHEST, preferred_element_type=F32
        )
    det1[j] = part
    each(1, nc, lambda k: col_copy(k, det1.at[j], det1.at[j], d1_ss, d1_rs, k).start())

    pot_in[0] = pot_out[j // 4]
    each(1, nc, lambda k: plain_wait(k, pot_in, pot_rs))
    pot = jnp.sum(pot_in[...].astype(F32), axis=0)
    pot = pltpu.roll(pot, lax.rem(128 - FD * lax.rem(j, 4), 128), 1)
    pot_o[...] = pot[:, 0:FD].astype(BF16)

    each(1, nc, lambda k: plain_wait(k, det1, d1_rs))
    det2[i] = jnp.sum(det1[...], axis=0)
    for k in range(nr - 1, 0, -1):
        row_copy(k, det2.at[i], det2.at[i], d2_ss, d2_rs).start()
    each(1, nr, lambda k: plain_wait(k, det2, d2_rs))
    det_o[...] = jnp.sum(det2[...], axis=0) * wave_scale

    def sent(n, buf, ss):
        def wait(k):
            pltpu.make_async_remote_copy(
                src_ref=buf.at[0], dst_ref=buf.at[0], send_sem=ss.at[k], recv_sem=ss.at[k],
                device_id=(i, j), device_id_type=MESH,
            ).wait_send()

        each(1, n, wait)

    sent(nc, tgt, tgt_ss)
    sent(nr, src, src_ss)
    sent(nc, fgs, fg_ss)
    sent(nc, rs_out, rs_ss)
    sent(nr, den, den_ss)
    sent(nc, pot_out, pot_ss)
    sent(nc, det1, d1_ss)
    sent(nr, det2, d2_ss)


def local(
    nz, ny, nc, panel_xyz, panel_weight, self_term, panel_slot, block_inverse, incident, field_xyz, field_group
):
    nr = nz * ny
    panels = SH * nr * nc
    fields = field_xyz.shape[1]
    scale = CYCLES * B3 / math.sqrt(panels)
    wave_scale = 1.0 / math.sqrt(fields * nr / GROUPS)
    sel_b, sel_a = selectors()
    vmem, dma = pltpu.VMEM, pltpu.SemaphoreType.DMA
    whole = pl.BlockSpec(memory_space=pltpu.VMEM)
    sems = []
    for n in (nr, nc, nc, nr, nc, nc, nc, nr):
        sems += [dma((n,)), dma((n,))]
    return pl.pallas_call(
        functools.partial(kernel, nz, ny, nc, scale, wave_scale),
        out_shape=(
            jax.ShapeDtypeStruct((WV, SH), F32),
            jax.ShapeDtypeStruct((WV, FD), BF16),
            jax.ShapeDtypeStruct((WV, GROUPS), F32),
        ),
        in_specs=[whole] * 10,
        out_specs=(whole,) * 3,
        scratch_shapes=[
            vmem((16, SH), F32),
            vmem((16, fields), F32),
            vmem((8, 128), F32),
            vmem((nr, 32, SH), BF16),
            vmem((nc, 16, SH), BF16),
            vmem((32, nc * SH), BF16),
            vmem((32, fields), BF16),
            vmem((SH, SH), F32),
            vmem((WV, nc * SH), F32),
            vmem((nc, WV, SH), BF16),
            vmem((nc, WV, SH), BF16),
            vmem((nr, WV, SH), BF16),
            vmem((nr // 2, 2 * SH, fields), BF16),
            vmem((WV, fields), F32),
            vmem((fields // 128, WV, 128), BF16),
            vmem((nc, WV, 128), BF16),
            vmem((nc, 8, 128), F32),
            vmem((nc, WV, GROUPS), F32),
            vmem((nr, WV, GROUPS), F32),
        ] + sems,
        compiler_params=pltpu.CompilerParams(
            collective_id=0, has_side_effects=True, vmem_limit_bytes=48 * 1024 * 1024
        ),
    )(
        panel_xyz, panel_weight, self_term.reshape(1, SH), panel_slot.reshape(1, SH), block_inverse, incident,
        field_xyz, field_group.reshape(1, FD), jnp.asarray(sel_b, BF16), jnp.asarray(sel_a, BF16),
    )


def solution(mesh):
    nr, nc = mesh.shape["row"], mesh.shape["col"]
    ny = 4 if nr % 8 == 0 else 2
    return jax.shard_map(
        functools.partial(local, nr // ny, ny, nc),
        mesh=mesh,
        in_specs=(
            P(None, ("col", "row")),
            P(None, ("col", "row")),
            P(("col", "row")),
            P(("col", "row")),
            P(None, ("col", "row")),
            P(None, ("col", "row")),
            P(None, "row"),
            P(("row", "col")),
        ),
        out_specs=(P(None, ("col", "row")), P(None, ("row", "col")), P()),
        check_vma=False,
    )
```

```python
import functools
import math

import jax
import jax.numpy as jnp
import numpy as np
from jax import lax
from jax.experimental import pallas as pl
from jax.experimental.pallas import tpu as pltpu
from jax.sharding import PartitionSpec as P

MESH = pl.DeviceIdType.MESH
HIGHEST = lax.Precision.HIGHEST
F32 = jnp.float32
BF16 = jnp.bfloat16

GROUPS = 128
SH = 128
WV = 16
FD = 32
wave_number = 12.0
smoothing = 0.05
damping = 0.5

B0, B1, B2, B3 = 6.283164041181243, -41.33714186520903, 81.3407492682057, -70.99322232997507
CYCLES = wave_number / (2.0 * math.pi)
EPS = smoothing * smoothing * CYCLES * CYCLES


def selectors():
    sel_b = np.zeros((16, 32), np.float32)
    sel_a = np.zeros((32, 16), np.float32)
    high, mid, low = 0, 1, 2
    pairs = [(high, high), (high, mid), (mid, high), (mid, mid), (high, low), (low, high), (mid, low), (low, mid)]
    k = 0
    for b, a in pairs:
        for c in range(3):
            sel_b[3 * b + c, k] = -2.0
            sel_a[k, 3 * a + c] = 1.0
            k += 1
    for n in range(3):
        sel_b[9 + n, k] = 1.0
        sel_a[k, 12] = 1.0
        k += 1
    for n in range(3):
        sel_b[12, k] = 1.0
        sel_a[k, 9 + n] = 1.0
        k += 1
    return sel_b, sel_a


def split3(x):
    h = x.astype(BF16).astype(F32)
    m = (x - h).astype(BF16).astype(F32)
    return h, m, (x - h) - m


def pieces(coords):
    parts = [split3(c) for c in coords]
    norm = split3(coords[0] * coords[0] + coords[1] * coords[1] + coords[2] * coords[2])
    rows = [parts[c][p] for p in range(3) for c in range(3)]
    return rows + list(norm) + [jnp.ones_like(norm[0])]


def pair_values(d):
    s = jnp.maximum(d, 1e-12)
    r = s * lax.rsqrt(s)
    v = 0.25 - jnp.abs(r - jnp.round(r))
    q = v * v
    p = ((q + B2 / B3) * q + B1 / B3) * q + B0 / B3
    return ((p * v) * lax.rsqrt(s + EPS)).astype(BF16)


def kernel(
    nz, ny, nc, scale, wave_scale,
    xyz_h, weight_h, self_h, slot_h, binv_h, inc_h, fxyz_h, fgroup_h, sel_b_h, sel_a_h,
    den_o, pot_o, det_o,
    xyz, weight, self_term, slot, binv, inc, fxyz, fgroup, sel_b, sel_a,
    geo_s, fs, src, tgt, feat_a, xt, coupled, acc, rsr_out, rsr_in, rs_out, rs_in, fpk, fgeo, onehot,
    den, gf, facc, pot_out, pot_in, det1, det2,
    load_s, src_ss, src_rs, tgt_ss, tgt_rs, rsr_ss, rsr_rs, rs_ss, rs_rs, den_ss, den_rs, fpk_ss, fpk_rs,
    pot_ss, pot_rs, d1_ss, d1_rs, d2_ss, d2_rs,
):
    nr = nz * ny
    i = lax.axis_index("row")
    j = lax.axis_index("col")
    iz, iy = i // ny, i % ny
    order, two_way, own = plan(nz, ny)
    chunks = len(order) // 2

    def each(lo, hi, body):
        def step(n, _):
            body(n)
            return 0

        lax.fori_loop(lo, hi, step, 0)

    barrier = pltpu.get_barrier_semaphore()
    each(1, nr, lambda n: pl.semaphore_signal(
        barrier, inc=1, device_id=(lax.rem(i + n, nr), j), device_id_type=MESH))
    each(1, nc, lambda n: pl.semaphore_signal(
        barrier, inc=1, device_id=(i, lax.rem(j + n, nc)), device_id_type=MESH))

    loads = [
        pltpu.make_async_copy(a, b, load_s.at[n])
        for n, (a, b) in enumerate([
            (xyz_h, xyz), (weight_h, weight), (self_h, self_term), (slot_h, slot), (binv_h, binv), (inc_h, inc),
            (fxyz_h, fxyz), (fgroup_h, fgroup), (sel_b_h, sel_b), (sel_a_h, sel_a),
        ])
    ]
    for load in loads:
        load.start()
    for load in loads:
        load.wait()

    rows = pieces([xyz[c:c + 1, :] * CYCLES for c in range(3)])
    for n, row in enumerate(rows):
        geo_s[n:n + 1, :] = row
    geo_s[13:16, :] = jnp.zeros((3, SH), F32)
    packet = geo_s[...].astype(BF16)
    src[own, 0:16, :] = packet
    tgt[0, 0:16, :] = packet
    place = lax.broadcasted_iota(jnp.int32, (64, SH), 0)
    chosen = (place == slot[...] % 64).astype(F32)
    half = (lax.broadcasted_iota(jnp.int32, (8, SH), 0) == slot[...] // 64).astype(F32)
    over_rows = (((0,), (0,)), ((), ()))
    over_lanes = (((1,), (1,)), ((), ()))
    picked = lax.dot_general(binv[...], chosen, over_rows, precision=HIGHEST, preferred_element_type=F32)
    same = lax.dot_general(half, half, over_rows, preferred_element_type=F32)
    coupled[...] = picked * same

    def precondition(values):
        mixing = jnp.dot(values, coupled[...], precision=HIGHEST, preferred_element_type=F32)
        return values / self_term[...] + mixing

    start = precondition(inc[...])
    start_w = (start * weight[...]).astype(BF16)
    src[own, 16:32, :] = start_w
    tgt[0, 16:32, :] = start_w

    lane = lax.broadcasted_iota(jnp.int32, (8, 128), 1)
    fs[...] = jnp.zeros_like(fs)
    fs[0, 0:3, :] = fxyz[:, pl.ds(pl.multiple_of(j // 4 * 128, 128), 128)]
    fs[1, 0:1, 0:FD] = fgroup[...].astype(F32)
    points = pltpu.roll(fs[0], lax.rem(128 - FD * lax.rem(j, 4), 128), 1)
    points = jnp.where(lane < FD, points, 0.0)
    row = points[0:1] + pltpu.roll(points, FD, 1)[1:2] + pltpu.roll(points, 2 * FD, 1)[2:3]
    row = row + pltpu.roll(fs[1], 3 * FD, 1)[0:1]
    mine = iy * nz + iz
    fpk[mine] = row

    pl.semaphore_wait(barrier, nr + nc - 2)

    def row_copy(d, k, src_ref, dst_ref, ss, rs):
        dz, dy = d
        peer = lax.rem(iz + dz % nz, nz) * ny + lax.rem(iy + dy % ny, ny)
        return pltpu.make_async_remote_copy(
            src_ref=src_ref, dst_ref=dst_ref, send_sem=ss.at[k], recv_sem=rs.at[k],
            device_id=(peer, j), device_id_type=MESH,
        )

    def col_copy(k, src_ref, dst_ref, ss, rs):
        return pltpu.make_async_remote_copy(
            src_ref=src_ref, dst_ref=dst_ref, send_sem=ss.at[k], recv_sem=rs.at[k],
            device_id=(i, lax.rem(j + k, nc)), device_id_type=MESH,
        )

    def arrived(k, buf, rs):
        pltpu.make_async_remote_copy(
            src_ref=buf.at[0], dst_ref=buf.at[0], send_sem=rs.at[k], recv_sem=rs.at[k],
            device_id=(i, j), device_id_type=MESH,
        ).wait_recv()

    each(1, nc, lambda k: col_copy(k, tgt.at[0], tgt.at[k], tgt_ss, tgt_rs).start())
    for k, (dz, dy) in enumerate(order):
        if k != own:
            row_copy((-dz, -dy), k, src.at[own], src.at[k], src_ss, src_rs).start()
    others = [(dz, dy) for dz in range(nz) for dy in range(ny)][1:]
    for k, d in enumerate(others):
        row_copy(d, k, fpk.at[mine], fpk.at[mine], fpk_ss, fpk_rs).start()

    def features_a(pk):
        return jnp.dot(sel_a[...], pk, preferred_element_type=F32).astype(BF16)

    def features_b(pk):
        return lax.dot_general(pk, sel_b[...], over_rows, preferred_element_type=F32).astype(BF16)

    acc[...] = jnp.zeros_like(acc)

    def take_target(k):
        cols = pl.ds(pl.multiple_of(k * SH, SH), SH)
        feat_a[:, cols] = features_a(tgt[k, 0:16, :])
        xt[:, cols] = tgt[k, 16:32, :]

    take_target(0)

    def next_target(k):
        arrived(k, tgt, tgt_rs)
        take_target(k)

    each(1, nc, next_target)

    def images_chunk(c):
        @pl.when(c != own // 2)
        def _():
            arrived(2 * c, src, src_rs)

        arrived(2 * c + 1, src, src_rs)
        one, two = src[2 * c], src[2 * c + 1]
        b = features_b(jnp.concatenate([one[0:16], two[0:16]], axis=1))
        x = jnp.concatenate([one[16:32], two[16:32]], axis=1)
        g = pair_values(jnp.dot(b, feat_a[...], preferred_element_type=F32))
        acc[...] += jnp.dot(x, g, preferred_element_type=F32)
        back = lax.dot_general(xt[...], g, over_lanes, preferred_element_type=F32).astype(BF16)
        rsr_out[2 * c] = back[:, 0:SH]
        rsr_out[2 * c + 1] = back[:, SH:2 * SH]
        for k in two_way:
            @pl.when(c == k // 2)
            def _():
                row_copy(order[k], k, rsr_out.at[k], rsr_in.at[k], rsr_ss, rsr_rs).start()

    each(0, chunks, images_chunk)

    def rs_send(k):
        rs_out[k] = acc[:, pl.ds(pl.multiple_of(k * SH, SH), SH)].astype(BF16)
        pltpu.make_async_remote_copy(
            src_ref=rs_out.at[k], dst_ref=rs_in.at[k], send_sem=rs_ss.at[k], recv_sem=rs_rs.at[k],
            device_id=(i, lax.rem(j + nc - k, nc)), device_id_type=MESH,
        ).start()

    each(1, nc, rs_send)

    each(0, nr - 1, lambda k: arrived(k, fpk, fpk_rs))
    packets = fpk[...].reshape(nr, 128)
    quarter = lax.broadcasted_iota(jnp.int32, (nz, 128), 1) // FD
    comps = []
    for c in range(4):
        comp = jnp.zeros((nz, 128), F32)
        for a in range(ny):
            moved = packets[a * nz:(a + 1) * nz]
            if a != c:
                moved = pltpu.roll(moved, FD * (a - c) % 128, 1)
            comp = jnp.where(quarter == a, moved, comp)
        comps.append(comp)
    frows = pieces([comp * CYCLES for comp in comps[:3]])
    detectors = lax.broadcasted_iota(jnp.int32, (GROUPS, 128), 0).astype(F32)
    for m in range(nz):
        for n, part in enumerate(frows):
            fgeo[m, n:n + 1, :] = part[m:m + 1]
        fgeo[m, 13:16, :] = jnp.zeros((3, 128), F32)
        onehot[:, m * 128:(m + 1) * 128] = (detectors == comps[3][m:m + 1]).astype(BF16)

    def field_chunk(c):
        b = features_b(jnp.concatenate([fgeo[2 * c], fgeo[2 * c + 1]], axis=1).astype(BF16))
        g = pair_values(jnp.dot(b, feat_a[...], preferred_element_type=F32))
        for q in range(nc // 2):
            gf[q, pl.ds(pl.multiple_of(c * 256, 256), 256), :] = g[:, q * 256:(q + 1) * 256]

    early = nz // 4
    each(0, early, field_chunk)

    rs_in[0] = jnp.zeros((WV, SH), BF16)
    total = acc[:, 0:SH]
    each(1, nc, lambda k: arrived(k, rs_in, rs_rs))
    total = total + jnp.sum(rs_in[...].astype(F32), axis=0)
    for k in two_way:
        arrived(k, rsr_in, rsr_rs)
        total = total + rsr_in[k].astype(F32)
    residual = inc[...] - self_term[...] * start - total * scale
    density = start + damping * precondition(residual)
    den_o[...] = density
    den[0] = (density * weight[...]).astype(BF16)
    each(1, nc, lambda k: col_copy(k, den.at[0], den.at[k], den_ss, den_rs).start())

    each(early, nz // 2, field_chunk)
    facc[...] = jnp.zeros_like(facc)

    def field_sum(q):
        @pl.when(q > 0)
        def _():
            arrived(2 * q, den, den_rs)

        arrived(2 * q + 1, den, den_rs)
        x = jnp.concatenate([den[2 * q], den[2 * q + 1]], axis=1)
        facc[...] += lax.dot_general(x, gf[q], over_lanes, preferred_element_type=F32)

    each(0, nc // 2, field_sum)

    fsum = facc[...] * scale
    h, m, l = split3(fsum)
    parts = jnp.concatenate([h.astype(BF16), m.astype(BF16), l.astype(BF16)], axis=0)
    sums = lax.dot_general(parts, onehot[...], over_lanes, preferred_element_type=F32)
    det1[j] = sums[0:WV] + sums[WV:2 * WV] + sums[2 * WV:3 * WV]
    each(1, nc, lambda k: col_copy(k, det1.at[j], det1.at[j], d1_ss, d1_rs).start())

    for m in range(nz):
        pot_out[m] = fsum[:, m * 128:(m + 1) * 128].astype(BF16)
    for k, d in enumerate(others):
        row_copy(d, k, pot_out.at[lax.rem(iz + d[0], nz)], pot_in.at[k], pot_ss, pot_rs).start()

    each(1, nc, lambda k: arrived(k, det1, d1_rs))
    det2[i] = jnp.sum(det1[...], axis=0)
    for k, d in enumerate(others):
        row_copy(d, k, det2.at[i], det2.at[i], d2_ss, d2_rs).start()

    each(0, nr - 1, lambda k: arrived(k, pot_in, pot_rs))
    pot_in[nr - 1] = pot_out[iz]
    pot = jnp.sum(pot_in[...].astype(F32), axis=0)
    pot = pltpu.roll(pot, lax.rem(128 - FD * iy, 128), 1)
    pot_o[...] = pot[:, 0:FD].astype(BF16)

    each(0, nr - 1, lambda k: arrived(k, det2, d2_rs))
    det_o[...] = jnp.sum(det2[...], axis=0) * wave_scale

    def sent(ks, buf, ss):
        def wait(k):
            pltpu.make_async_remote_copy(
                src_ref=buf.at[0], dst_ref=buf.at[0], send_sem=ss.at[k], recv_sem=ss.at[k],
                device_id=(i, j), device_id_type=MESH,
            ).wait_send()

        if isinstance(ks, range):
            each(ks.start, ks.stop, wait)
        else:
            for k in ks:
                wait(k)

    sent(range(1, nc), tgt, tgt_ss)
    sent(range(0, own), src, src_ss)
    sent(range(own + 1, len(order)), src, src_ss)
    sent(range(0, nr - 1), fpk, fpk_ss)
    sent(two_way, rsr_out, rsr_ss)
    sent(range(1, nc), rs_out, rs_ss)
    sent(range(1, nc), den, den_ss)
    sent(range(0, nr - 1), pot_out, pot_ss)
    sent(range(1, nc), det1, d1_ss)
    sent(range(0, nr - 1), det2, d2_ss)


def plan(nz, ny):
    def hops(d):
        return min(d[0], nz - d[0]) + 2 * min(d[1], ny - d[1])

    both = [(dz, dy) for dy in range(1, ny // 2) for dz in range(nz)]
    both += [(dz, dy) for dy in (0, ny // 2) for dz in range(1, nz // 2)]
    both = sorted(both, key=hops)
    pairs = [both[n:n + 2] for n in range(0, len(both), 2)]
    near = pairs[:len(pairs) // 2]
    far = pairs[len(pairs) // 2:][::-1]
    home = [(0, 0), (0, ny // 2)]
    last = [(nz // 2, 0), (nz // 2, ny // 2)]
    seq = near[:1] + [home] + near[1:] + far + [last]
    order = [d for pair in seq for d in pair]
    two_way = [k for k, d in enumerate(order) if d in both]
    return order, two_way, order.index((0, 0))


def local(
    nz, ny, nc, panel_xyz, panel_weight, self_term, panel_slot, block_inverse, incident, field_xyz, field_group
):
    nr = nz * ny
    panels = SH * nr * nc
    fields = field_xyz.shape[1]
    mine = nz * 128
    scale = CYCLES * B3 / math.sqrt(panels)
    wave_scale = 1.0 / math.sqrt(fields * nr / GROUPS)
    sel_b, sel_a = selectors()
    slots = len(plan(nz, ny)[0])
    vmem, dma = pltpu.VMEM, pltpu.SemaphoreType.DMA
    sems = [dma((10,))]
    for n in (slots, nc, slots, nc, nc, nr, nr, nc, nr):
        sems += [dma((n,)), dma((n,))]
    args = (
        panel_xyz, panel_weight, self_term.reshape(1, SH), panel_slot.reshape(1, SH), block_inverse, incident,
        field_xyz, field_group.reshape(1, FD), jnp.asarray(sel_b, BF16), jnp.asarray(sel_a, BF16),
    )
    return pl.pallas_call(
        functools.partial(kernel, nz, ny, nc, scale, wave_scale),
        out_shape=(
            jax.ShapeDtypeStruct((WV, SH), F32),
            jax.ShapeDtypeStruct((WV, FD), BF16),
            jax.ShapeDtypeStruct((WV, GROUPS), F32),
        ),
        in_specs=[pl.BlockSpec(memory_space=pltpu.HBM)] * 10,
        out_specs=(pl.BlockSpec(memory_space=pltpu.VMEM),) * 3,
        scratch_shapes=[vmem(a.shape, a.dtype) for a in args] + [
            vmem((16, SH), F32),
            vmem((2, 8, 128), F32),
            vmem((slots, 32, SH), BF16),
            vmem((nc, 32, SH), BF16),
            vmem((32, nc * SH), BF16),
            vmem((WV, nc * SH), BF16),
            vmem((SH, SH), F32),
            vmem((WV, nc * SH), F32),
            vmem((slots, WV, SH), BF16),
            vmem((slots, WV, SH), BF16),
            vmem((nc, WV, SH), BF16),
            vmem((nc, WV, SH), BF16),
            vmem((nr, 1, 128), F32),
            vmem((nz, 16, 128), F32),
            vmem((GROUPS, mine), BF16),
            vmem((nc, WV, SH), BF16),
            vmem((nc // 2, mine, 256), BF16),
            vmem((WV, mine), F32),
            vmem((nz, WV, 128), BF16),
            vmem((nr, WV, 128), BF16),
            vmem((nc, WV, GROUPS), F32),
            vmem((nr, WV, GROUPS), F32),
        ] + sems,
        compiler_params=pltpu.CompilerParams(
            collective_id=0, has_side_effects=True, vmem_limit_bytes=48 * 1024 * 1024
        ),
    )(*args)


def solution(mesh):
    nr, nc = mesh.shape["row"], mesh.shape["col"]
    ny = 4
    return jax.shard_map(
        functools.partial(local, nr // ny, ny, nc),
        mesh=mesh,
        in_specs=(
            P(None, ("col", "row")),
            P(None, ("col", "row")),
            P(("col", "row")),
            P(("col", "row")),
            P(None, ("col", "row")),
            P(None, ("col", "row")),
            P(None, "row"),
            P(("row", "col")),
        ),
        out_specs=(P(None, ("col", "row")), P(None, ("row", "col")), P()),
        check_vma=False,
    )
```

```python
import functools
import math

import jax
import jax.numpy as jnp
import numpy as np
from jax import lax
from jax.experimental import pallas as pl
from jax.experimental.pallas import tpu as pltpu
from jax.sharding import PartitionSpec as P

MESH = pl.DeviceIdType.MESH
HIGHEST = lax.Precision.HIGHEST
F32 = jnp.float32
BF16 = jnp.bfloat16

GROUPS = 128
SH = 128
WV = 16
FD = 32
wave_number = 12.0
smoothing = 0.05
damping = 0.5

B0, B1, B2, B3 = 6.283164041181243, -41.33714186520903, 81.3407492682057, -70.99322232997507
CYCLES = wave_number / (2.0 * math.pi)
EPS = smoothing * smoothing * CYCLES * CYCLES


def selectors():
    sel_b = np.zeros((16, 32), np.float32)
    sel_a = np.zeros((32, 16), np.float32)
    high, mid, low = 0, 1, 2
    pairs = [(high, high), (high, mid), (mid, high), (mid, mid), (high, low), (low, high), (mid, low), (low, mid)]
    k = 0
    for b, a in pairs:
        for c in range(3):
            sel_b[3 * b + c, k] = -2.0
            sel_a[k, 3 * a + c] = 1.0
            k += 1
    for n in range(3):
        sel_b[9 + n, k] = 1.0
        sel_a[k, 12] = 1.0
        k += 1
    for n in range(3):
        sel_b[12, k] = 1.0
        sel_a[k, 9 + n] = 1.0
        k += 1
    return sel_b, sel_a


def split3(x):
    h = x.astype(BF16).astype(F32)
    m = (x - h).astype(BF16).astype(F32)
    return h, m, (x - h) - m


def pieces(coords):
    parts = [split3(c) for c in coords]
    norm = split3(coords[0] * coords[0] + coords[1] * coords[1] + coords[2] * coords[2])
    rows = [parts[c][p] for p in range(3) for c in range(3)]
    return rows + list(norm) + [jnp.ones_like(norm[0])]


def pair_values(d):
    s = jnp.maximum(d, 1e-12)
    r = s * lax.rsqrt(s)
    v = 0.25 - jnp.abs(r - jnp.round(r))
    q = v * v
    p = ((q + B2 / B3) * q + B1 / B3) * q + B0 / B3
    return ((p * v) * lax.rsqrt(s + EPS)).astype(BF16)


def kernel(
    nz, ny, nc, scale, wave_scale,
    xyz_h, weight_h, self_h, slot_h, binv_h, inc_h, fxyz_h, fgroup_h, sel_b_h, sel_a_h,
    den_o, pot_o, det_o,
    xyz, weight, self_term, slot, binv, inc, fxyz, fgroup, sel_b, sel_a,
    geo_s, fs, src, tgt, feat_a, xt, coupled, acc, gbuf, rsr_out, rsr_in, rs_out, rs_in, fpk, fgeo, onehot,
    den, gf, facc, pot_out, pot_in, detp, det1, det2, det3,
    load_s, src_ss, src_rs, tgt_ss, tgt_rs, rsr_ss, rsr_rs, rs_ss, rs_rs, den_ss, den_rs, fpk_ss, fpk_rs,
    pot_ss, pot_rs, d1_ss, d1_rs, d2_ss, d2_rs, d3_s,
):
    nr = nz * ny
    i = lax.axis_index("row")
    j = lax.axis_index("col")
    iz, iy = i // ny, i % ny
    order, two_way, own = plan(nz, ny)
    chunks = len(order) // 2

    def each(lo, hi, body):
        def step(n, _):
            body(n)
            return 0

        lax.fori_loop(lo, hi, step, 0)

    barrier = pltpu.get_barrier_semaphore()
    each(1, nr, lambda n: pl.semaphore_signal(
        barrier, inc=1, device_id=(lax.rem(i + n, nr), j), device_id_type=MESH))
    each(1, nc, lambda n: pl.semaphore_signal(
        barrier, inc=1, device_id=(i, lax.rem(j + n, nc)), device_id_type=MESH))

    loads = [
        pltpu.make_async_copy(a, b, load_s.at[n])
        for n, (a, b) in enumerate([
            (xyz_h, xyz), (weight_h, weight), (self_h, self_term), (slot_h, slot), (binv_h, binv), (inc_h, inc),
            (fxyz_h, fxyz), (fgroup_h, fgroup), (sel_b_h, sel_b), (sel_a_h, sel_a),
        ])
    ]
    for load in loads:
        load.start()
    for load in loads:
        load.wait()

    rows = pieces([xyz[c:c + 1, :] * CYCLES for c in range(3)])
    for n, row in enumerate(rows):
        geo_s[n:n + 1, :] = row
    geo_s[13:16, :] = jnp.zeros((3, SH), F32)
    packet = geo_s[...].astype(BF16)
    src[own, 0:16, :] = packet
    tgt[0, 0:16, :] = packet
    place = lax.broadcasted_iota(jnp.int32, (64, SH), 0)
    chosen = (place == slot[...] % 64).astype(F32)
    half = (lax.broadcasted_iota(jnp.int32, (8, SH), 0) == slot[...] // 64).astype(F32)
    over_rows = (((0,), (0,)), ((), ()))
    over_lanes = (((1,), (1,)), ((), ()))
    picked = lax.dot_general(binv[...], chosen, over_rows, precision=HIGHEST, preferred_element_type=F32)
    same = lax.dot_general(half, half, over_rows, preferred_element_type=F32)
    coupled[...] = picked * same

    def precondition(values):
        mixing = jnp.dot(values, coupled[...], precision=HIGHEST, preferred_element_type=F32)
        return values / self_term[...] + mixing

    start = precondition(inc[...])
    start_w = (start * weight[...]).astype(BF16)
    src[own, 16:32, :] = start_w
    tgt[0, 16:32, :] = start_w

    lane = lax.broadcasted_iota(jnp.int32, (8, 128), 1)
    fs[...] = jnp.zeros_like(fs)
    fs[0, 0:3, :] = fxyz[:, pl.ds(pl.multiple_of(j // 4 * 128, 128), 128)]
    fs[1, 0:1, 0:FD] = fgroup[...].astype(F32)
    points = pltpu.roll(fs[0], lax.rem(128 - FD * lax.rem(j, 4), 128), 1)
    points = jnp.where(lane < FD, points, 0.0)
    row = points[0:1] + pltpu.roll(points, FD, 1)[1:2] + pltpu.roll(points, 2 * FD, 1)[2:3]
    row = row + pltpu.roll(fs[1], 3 * FD, 1)[0:1]
    mine = iy * nz + iz
    fpk[mine] = row

    pl.semaphore_wait(barrier, nr + nc - 2)

    def row_copy(d, k, src_ref, dst_ref, ss, rs):
        dz, dy = d
        peer = lax.rem(iz + dz % nz, nz) * ny + lax.rem(iy + dy % ny, ny)
        return pltpu.make_async_remote_copy(
            src_ref=src_ref, dst_ref=dst_ref, send_sem=ss.at[k], recv_sem=rs.at[k],
            device_id=(peer, j), device_id_type=MESH,
        )

    def col_copy(k, src_ref, dst_ref, ss, rs):
        return pltpu.make_async_remote_copy(
            src_ref=src_ref, dst_ref=dst_ref, send_sem=ss.at[k], recv_sem=rs.at[k],
            device_id=(i, lax.rem(j + k, nc)), device_id_type=MESH,
        )

    def arrived(k, buf, rs):
        pltpu.make_async_remote_copy(
            src_ref=buf.at[0], dst_ref=buf.at[0], send_sem=rs.at[k], recv_sem=rs.at[k],
            device_id=(i, j), device_id_type=MESH,
        ).wait_recv()

    each(1, nc, lambda k: col_copy(k, tgt.at[0], tgt.at[k], tgt_ss, tgt_rs).start())
    for k, (dz, dy) in enumerate(order):
        if k != own:
            row_copy((-dz, -dy), k, src.at[own], src.at[k], src_ss, src_rs).start()
    others = [(dz, dy) for dz in range(nz) for dy in range(ny)][1:]
    for k, d in enumerate(others):
        row_copy(d, k, fpk.at[mine], fpk.at[mine], fpk_ss, fpk_rs).start()

    def features_a(pk):
        return jnp.dot(sel_a[...], pk, preferred_element_type=F32).astype(BF16)

    def features_b(pk):
        return lax.dot_general(pk, sel_b[...], over_rows, preferred_element_type=F32).astype(BF16)

    acc[...] = jnp.zeros_like(acc)

    each(1, nc, lambda k: arrived(k, tgt, tgt_rs))
    for k in range(0, nc, 4):
        group = [tgt[n] for n in range(k, k + 4)]
        feat_a[:, k * SH:(k + 4) * SH] = features_a(jnp.concatenate([p[0:16] for p in group], axis=1))
        xt[:, k * SH:(k + 4) * SH] = jnp.concatenate([p[16:32] for p in group], axis=1)

    def tile(c):
        b = features_b(jnp.concatenate([src[2 * c, 0:16, :], src[2 * c + 1, 0:16, :]], axis=1))
        gbuf[...] = pair_values(jnp.dot(b, feat_a[...], preferred_element_type=F32))

    def use(c):
        x = jnp.concatenate([src[2 * c, 16:32, :], src[2 * c + 1, 16:32, :]], axis=1)
        g = gbuf[...]
        acc[...] += jnp.dot(x, g, preferred_element_type=F32)
        back = lax.dot_general(xt[...], g, over_lanes, preferred_element_type=F32).astype(BF16)
        rsr_out[2 * c] = back[:, 0:SH]
        rsr_out[2 * c + 1] = back[:, SH:2 * SH]

    def wait_chunk(c):
        @pl.when(c != own // 2)
        def _():
            arrived(2 * c, src, src_rs)

        arrived(2 * c + 1, src, src_rs)

    def images_chunk(c):
        wait_chunk(c)
        use(c - 1)
        tile(c)
        for k in two_way:
            @pl.when(c - 1 == k // 2)
            def _():
                row_copy(order[k], k, rsr_out.at[k], rsr_in.at[k], rsr_ss, rsr_rs).start()

    wait_chunk(0)
    tile(0)
    each(1, chunks, images_chunk)
    use(chunks - 1)

    def rs_send(k):
        rs_out[k] = acc[:, pl.ds(pl.multiple_of(k * SH, SH), SH)].astype(BF16)
        pltpu.make_async_remote_copy(
            src_ref=rs_out.at[k], dst_ref=rs_in.at[k], send_sem=rs_ss.at[k], recv_sem=rs_rs.at[k],
            device_id=(i, lax.rem(j + nc - k, nc)), device_id_type=MESH,
        ).start()

    each(1, nc, rs_send)

    each(0, nr - 1, lambda k: arrived(k, fpk, fpk_rs))
    packets = fpk[...].reshape(nr, 128)
    quarter = lax.broadcasted_iota(jnp.int32, (nz, 128), 1) // FD
    comps = []
    for c in range(4):
        comp = jnp.zeros((nz, 128), F32)
        for a in range(ny):
            moved = packets[a * nz:(a + 1) * nz]
            if a != c:
                moved = pltpu.roll(moved, FD * (a - c) % 128, 1)
            comp = jnp.where(quarter == a, moved, comp)
        comps.append(comp)
    frows = pieces([comp * CYCLES for comp in comps[:3]])
    detectors = lax.broadcasted_iota(jnp.int32, (GROUPS, 128), 0).astype(F32)
    for m in range(nz):
        for n, part in enumerate(frows):
            fgeo[m, n:n + 1, :] = part[m:m + 1]
        fgeo[m, 13:16, :] = jnp.zeros((3, 128), F32)
        onehot[:, m * 128:(m + 1) * 128] = (detectors == comps[3][m:m + 1]).astype(BF16)

    def field_chunk(c):
        b = features_b(jnp.concatenate([fgeo[2 * c], fgeo[2 * c + 1]], axis=1).astype(BF16))
        g = pair_values(jnp.dot(b, feat_a[...], preferred_element_type=F32))
        for q in range(nc // 2):
            gf[q, pl.ds(pl.multiple_of(c * 256, 256), 256), :] = g[:, q * 256:(q + 1) * 256]

    early = nz // 4
    each(0, early, field_chunk)

    rs_in[0] = jnp.zeros((WV, SH), BF16)
    total = acc[:, 0:SH]
    each(1, nc, lambda k: arrived(k, rs_in, rs_rs))
    total = total + jnp.sum(rs_in[...].astype(F32), axis=0)
    for k in two_way:
        arrived(k, rsr_in, rsr_rs)
        total = total + rsr_in[k].astype(F32)
    residual = inc[...] - self_term[...] * start - total * scale
    density = start + damping * precondition(residual)
    den_o[...] = density
    den[0] = (density * weight[...]).astype(BF16)
    each(1, nc, lambda k: col_copy(k, den.at[0], den.at[k], den_ss, den_rs).start())

    each(early, nz // 2, field_chunk)
    facc[...] = jnp.zeros_like(facc)

    def field_sum(q):
        @pl.when(q > 0)
        def _():
            arrived(2 * q, den, den_rs)

        arrived(2 * q + 1, den, den_rs)
        x = jnp.concatenate([den[2 * q], den[2 * q + 1]], axis=1)
        facc[...] += lax.dot_general(x, gf[q], over_lanes, preferred_element_type=F32)

    each(0, nc // 2, field_sum)

    fsum = facc[...] * scale
    h, m, l = split3(fsum)
    parts = jnp.concatenate([h.astype(BF16), m.astype(BF16), l.astype(BF16)], axis=0)
    sums = lax.dot_general(parts, onehot[...], over_lanes, preferred_element_type=F32)
    detp[...] = sums[0:WV] + sums[WV:2 * WV] + sums[2 * WV:3 * WV]

    def waves_of(col):
        return pl.ds(pl.multiple_of(lax.rem(col, 2) * 8, 8), 8)

    each(1, nc, lambda k: col_copy(k, detp.at[waves_of(j + k)], det1.at[j], d1_ss, d1_rs).start())
    det1[j] = detp[waves_of(j), :]

    for m in range(nz):
        pot_out[m] = fsum[:, m * 128:(m + 1) * 128].astype(BF16)
    for k, d in enumerate(others):
        row_copy(d, k, pot_out.at[lax.rem(iz + d[0], nz)], pot_in.at[k], pot_ss, pot_rs).start()

    each(1, nc, lambda k: arrived(k, det1, d1_rs))
    det2[i] = jnp.sum(det1[...], axis=0)
    for k, d in enumerate(others):
        row_copy(d, k, det2.at[i], det2.at[i], d2_ss, d2_rs).start()

    each(0, nr - 1, lambda k: arrived(k, pot_in, pot_rs))
    pot_in[nr - 1] = pot_out[iz]
    pot = jnp.sum(pot_in[...].astype(F32), axis=0)
    pot = pltpu.roll(pot, lax.rem(128 - FD * iy, 128), 1)
    pot_o[...] = pot[:, 0:FD].astype(BF16)

    each(0, nr - 1, lambda k: arrived(k, det2, d2_rs))
    core = lax.rem(j, 2)
    det3[core] = jnp.sum(det2[...], axis=0) * wave_scale
    swap = pltpu.make_async_remote_copy(
        src_ref=det3.at[core], dst_ref=det3.at[core], send_sem=d3_s.at[0], recv_sem=d3_s.at[1],
        device_id=(i, j + 1 - 2 * core), device_id_type=MESH,
    )
    swap.start()
    swap.wait()
    det_o[...] = jnp.concatenate([det3[0], det3[1]], axis=0)

    def sent(ks, buf, ss):
        def wait(k):
            pltpu.make_async_remote_copy(
                src_ref=buf.at[0], dst_ref=buf.at[0], send_sem=ss.at[k], recv_sem=ss.at[k],
                device_id=(i, j), device_id_type=MESH,
            ).wait_send()

        if isinstance(ks, range):
            each(ks.start, ks.stop, wait)
        else:
            for k in ks:
                wait(k)

    sent(range(1, nc), tgt, tgt_ss)
    sent(range(0, own), src, src_ss)
    sent(range(own + 1, len(order)), src, src_ss)
    sent(range(0, nr - 1), fpk, fpk_ss)
    sent(two_way, rsr_out, rsr_ss)
    sent(range(1, nc), rs_out, rs_ss)
    sent(range(1, nc), den, den_ss)
    sent(range(0, nr - 1), pot_out, pot_ss)
    sent(range(1, nc), det1, d1_ss)
    sent(range(0, nr - 1), det2, d2_ss)


def plan(nz, ny):
    def hops(d):
        return min(d[0], nz - d[0]) + 2 * min(d[1], ny - d[1])

    both = [(dz, dy) for dy in range(1, ny // 2) for dz in range(nz)]
    both += [(dz, dy) for dy in (0, ny // 2) for dz in range(1, nz // 2)]
    both = sorted(both, key=hops)
    pairs = [both[n:n + 2] for n in range(0, len(both), 2)]
    near = pairs[:len(pairs) // 2]
    far = pairs[len(pairs) // 2:][::-1]
    home = [(0, 0), (0, ny // 2)]
    last = [(nz // 2, 0), (nz // 2, ny // 2)]
    seq = near[:1] + [home] + near[1:] + far + [last]
    order = [d for pair in seq for d in pair]
    two_way = [k for k, d in enumerate(order) if d in both]
    return order, two_way, order.index((0, 0))


def local(
    nz, ny, nc, panel_xyz, panel_weight, self_term, panel_slot, block_inverse, incident, field_xyz, field_group
):
    nr = nz * ny
    panels = SH * nr * nc
    fields = field_xyz.shape[1]
    mine = nz * 128
    scale = CYCLES * B3 / math.sqrt(panels)
    wave_scale = 1.0 / math.sqrt(fields * nr / GROUPS)
    sel_b, sel_a = selectors()
    slots = len(plan(nz, ny)[0])
    vmem, dma = pltpu.VMEM, pltpu.SemaphoreType.DMA
    sems = [dma((10,))]
    for n in (slots, nc, slots, nc, nc, nr, nr, nc, nr):
        sems += [dma((n,)), dma((n,))]
    sems += [dma((2,))]
    args = (
        panel_xyz, panel_weight, self_term.reshape(1, SH), panel_slot.reshape(1, SH), block_inverse, incident,
        field_xyz, field_group.reshape(1, FD), jnp.asarray(sel_b, BF16), jnp.asarray(sel_a, BF16),
    )
    return pl.pallas_call(
        functools.partial(kernel, nz, ny, nc, scale, wave_scale),
        out_shape=(
            jax.ShapeDtypeStruct((WV, SH), F32),
            jax.ShapeDtypeStruct((WV, FD), BF16),
            jax.ShapeDtypeStruct((WV, GROUPS), F32),
        ),
        in_specs=[pl.BlockSpec(memory_space=pltpu.HBM)] * 10,
        out_specs=(pl.BlockSpec(memory_space=pltpu.VMEM),) * 3,
        scratch_shapes=[vmem(a.shape, a.dtype) for a in args] + [
            vmem((16, SH), F32),
            vmem((2, 8, 128), F32),
            vmem((slots, 32, SH), BF16),
            vmem((nc, 32, SH), BF16),
            vmem((32, nc * SH), BF16),
            vmem((WV, nc * SH), BF16),
            vmem((SH, SH), F32),
            vmem((WV, nc * SH), F32),
            vmem((2 * SH, nc * SH), BF16),
            vmem((slots, WV, SH), BF16),
            vmem((slots, WV, SH), BF16),
            vmem((nc, WV, SH), BF16),
            vmem((nc, WV, SH), BF16),
            vmem((nr, 1, 128), F32),
            vmem((nz, 16, 128), F32),
            vmem((GROUPS, mine), BF16),
            vmem((nc, WV, SH), BF16),
            vmem((nc // 2, mine, 256), BF16),
            vmem((WV, mine), F32),
            vmem((nz, WV, 128), BF16),
            vmem((nr, WV, 128), BF16),
            vmem((WV, GROUPS), F32),
            vmem((nc, 8, GROUPS), F32),
            vmem((nr, 8, GROUPS), F32),
            vmem((2, 8, GROUPS), F32),
        ] + sems,
        compiler_params=pltpu.CompilerParams(
            collective_id=0, has_side_effects=True, vmem_limit_bytes=67043328
        ),
    )(*args)


def solution(mesh):
    nr, nc = mesh.shape["row"], mesh.shape["col"]
    ny = 4
    return jax.shard_map(
        functools.partial(local, nr // ny, ny, nc),
        mesh=mesh,
        in_specs=(
            P(None, ("col", "row")),
            P(None, ("col", "row")),
            P(("col", "row")),
            P(("col", "row")),
            P(None, ("col", "row")),
            P(None, ("col", "row")),
            P(None, "row"),
            P(("row", "col")),
        ),
        out_specs=(P(None, ("col", "row")), P(None, ("row", "col")), P()),
        check_vma=False,
    )
```

```python
import functools
import math

import jax
import jax.numpy as jnp
import numpy as np
from jax import lax
from jax.experimental import pallas as pl
from jax.experimental.pallas import tpu as pltpu
from jax.sharding import PartitionSpec as P

MESH = pl.DeviceIdType.MESH
HIGHEST = lax.Precision.HIGHEST
F32 = jnp.float32
BF16 = jnp.bfloat16

GROUPS = 128
SH = 128
WV = 16
FD = 32
wave_number = 12.0
smoothing = 0.05
damping = 0.5

LEAD, A1, A0 = 73.90290388562806, -0.5546875, 0.0849609375
CYCLES = wave_number / (2.0 * math.pi)
EPS = smoothing * smoothing * CYCLES * CYCLES


def selectors():
    sel_b = np.zeros((16, 32), np.float32)
    sel_a = np.zeros((32, 16), np.float32)
    high, mid, low = 0, 1, 2
    pairs = [(high, high), (high, mid), (mid, high), (mid, mid), (high, low), (low, high), (mid, low), (low, mid)]
    k = 0
    for b, a in pairs:
        for c in range(3):
            sel_b[3 * b + c, k] = -2.0
            sel_a[k, 3 * a + c] = 1.0
            k += 1
    for n in range(3):
        sel_b[9 + n, k] = 1.0
        sel_a[k, 12] = 1.0
        k += 1
    for n in range(3):
        sel_b[12, k] = 1.0
        sel_a[k, 9 + n] = 1.0
        k += 1
    return sel_b, sel_a


def split3(x):
    h = x.astype(BF16).astype(F32)
    m = (x - h).astype(BF16).astype(F32)
    return h, m, (x - h) - m


def pieces(coords):
    parts = [split3(c) for c in coords]
    norm = split3(coords[0] * coords[0] + coords[1] * coords[1] + coords[2] * coords[2])
    rows = [parts[c][p] for p in range(3) for c in range(3)]
    return rows + list(norm) + [jnp.ones_like(norm[0])]


def pair_values(d):
    s = jnp.maximum(d, 1e-12)
    r = s * lax.rsqrt(s)
    v = (0.25 - jnp.abs(r - jnp.round(r))).astype(BF16)
    q = v * v
    p = (q + BF16(A1)) * q + BF16(A0)
    return (p * v) * lax.rsqrt(s + EPS).astype(BF16)


def kernel(
    nz, ny, nc, scale, wave_scale,
    xyz_h, weight_h, self_h, slot_h, binv_h, inc_h, fxyz_h, fgroup_h, sel_b_h, sel_a_h,
    den_o, pot_o, det_o,
    xyz, weight, self_term, slot, binv, inc, fxyz, fgroup, sel_b, sel_a,
    geo_s, fs, src, tgt, tgx, feat_a, feat_b, feat_f, xt, coupled, acc, gbuf, rsr_out, rsr_in, rs_out, rs_in, fpk, fgeo, onehot,
    den, gf, facc, pot_out, pot_in, detp, det1, det2, det3,
    load_s, src_ss, src_rs, tgt_ss, tgt_rs, tgx_ss, tgx_rs, rsr_ss, rsr_rs, rs_ss, rs_rs, den_ss, den_rs, fpk_ss, fpk_rs,
    pot_ss, pot_rs, d1_ss, d1_rs, d2_ss, d2_rs, d3_s,
):
    nr = nz * ny
    i = lax.axis_index("row")
    j = lax.axis_index("col")
    iz, iy = i // ny, i % ny
    order, two_way, own = plan(nz, ny)
    chunks = len(order) // 2

    def each(lo, hi, body):
        def step(n, _):
            body(n)
            return 0

        lax.fori_loop(lo, hi, step, 0)

    barrier = pltpu.get_barrier_semaphore()
    each(1, nr, lambda n: pl.semaphore_signal(
        barrier, inc=1, device_id=(lax.rem(i + n, nr), j), device_id_type=MESH))
    each(1, nc, lambda n: pl.semaphore_signal(
        barrier, inc=1, device_id=(i, lax.rem(j + n, nc)), device_id_type=MESH))

    loads = [
        pltpu.make_async_copy(a, b, load_s.at[n])
        for n, (a, b) in enumerate([
            (xyz_h, xyz), (weight_h, weight), (self_h, self_term), (slot_h, slot), (binv_h, binv), (inc_h, inc),
            (fxyz_h, fxyz), (fgroup_h, fgroup), (sel_b_h, sel_b), (sel_a_h, sel_a),
        ])
    ]
    for load in loads:
        load.start()
    for load in loads:
        load.wait()

    rows = pieces([xyz[c:c + 1, :] * CYCLES for c in range(3)])
    for n, row in enumerate(rows):
        geo_s[n:n + 1, :] = row
    geo_s[13:16, :] = jnp.zeros((3, SH), F32)
    packet = geo_s[...].astype(BF16)
    src[own, 0:16, :] = packet
    tgt[0] = packet
    place = lax.broadcasted_iota(jnp.int32, (64, SH), 0)
    chosen = (place == slot[...] % 64).astype(F32)
    half = (lax.broadcasted_iota(jnp.int32, (8, SH), 0) == slot[...] // 64).astype(F32)
    over_rows = (((0,), (0,)), ((), ()))
    over_lanes = (((1,), (1,)), ((), ()))
    picked = lax.dot_general(binv[...], chosen, over_rows, precision=HIGHEST, preferred_element_type=F32)
    same = lax.dot_general(half, half, over_rows, preferred_element_type=F32)
    coupled[...] = picked * same

    def precondition(values):
        mixing = jnp.dot(values, coupled[...], precision=HIGHEST, preferred_element_type=F32)
        return values / self_term[...] + mixing

    start = precondition(inc[...])
    start_w = (start * weight[...]).astype(BF16)
    src[own, 16:32, :] = start_w
    tgx[0] = start_w

    lane = lax.broadcasted_iota(jnp.int32, (8, 128), 1)
    fs[...] = jnp.zeros_like(fs)
    fs[0, 0:3, :] = fxyz[:, pl.ds(pl.multiple_of(j // 4 * 128, 128), 128)]
    fs[1, 0:1, 0:FD] = fgroup[...].astype(F32)
    points = pltpu.roll(fs[0], lax.rem(128 - FD * lax.rem(j, 4), 128), 1)
    points = jnp.where(lane < FD, points, 0.0)
    row = points[0:1] + pltpu.roll(points, FD, 1)[1:2] + pltpu.roll(points, 2 * FD, 1)[2:3]
    row = row + pltpu.roll(fs[1], 3 * FD, 1)[0:1]
    mine = iy * nz + iz
    fpk[mine] = row

    pl.semaphore_wait(barrier, nr + nc - 2)

    def row_copy(d, k, src_ref, dst_ref, ss, rs):
        dz, dy = d
        peer = lax.rem(iz + dz % nz, nz) * ny + lax.rem(iy + dy % ny, ny)
        return pltpu.make_async_remote_copy(
            src_ref=src_ref, dst_ref=dst_ref, send_sem=ss.at[k], recv_sem=rs.at[k],
            device_id=(peer, j), device_id_type=MESH,
        )

    def col_copy(k, src_ref, dst_ref, ss, rs):
        return pltpu.make_async_remote_copy(
            src_ref=src_ref, dst_ref=dst_ref, send_sem=ss.at[k], recv_sem=rs.at[k],
            device_id=(i, lax.rem(j + k, nc)), device_id_type=MESH,
        )

    def arrived(k, buf, rs):
        pltpu.make_async_remote_copy(
            src_ref=buf.at[0], dst_ref=buf.at[0], send_sem=rs.at[k], recv_sem=rs.at[k],
            device_id=(i, j), device_id_type=MESH,
        ).wait_recv()

    each(1, nc, lambda k: col_copy(k, tgt.at[0], tgt.at[k], tgt_ss, tgt_rs).start())
    for k, (dz, dy) in enumerate(order):
        if k == 4:
            each(1, nc, lambda n: col_copy(n, tgx.at[0], tgx.at[n], tgx_ss, tgx_rs).start())
        if k != own:
            row_copy((-dz, -dy), k, src.at[own], src.at[k], src_ss, src_rs).start()
    others = [(dz, dy) for dz in range(nz) for dy in range(ny)][1:]
    for k, d in enumerate(others):
        row_copy(d, k, fpk.at[mine], fpk.at[mine], fpk_ss, fpk_rs).start()

    def features_a(pk):
        return jnp.dot(sel_a[...], pk, preferred_element_type=F32).astype(BF16)

    def features_b(pk):
        return lax.dot_general(pk, sel_b[...], over_rows, preferred_element_type=F32).astype(BF16)

    acc[...] = jnp.zeros_like(acc)

    each(1, nc, lambda k: arrived(k, tgt, tgt_rs))
    for k in range(0, nc, 4):
        feat_a[:, k * SH:(k + 4) * SH] = features_a(jnp.concatenate([tgt[n] for n in range(k, k + 4)], axis=1))

    def tile(b):
        return pair_values(jnp.dot(b, feat_a[...], preferred_element_type=F32))

    def source_features(c):
        return features_b(jnp.concatenate([src[2 * c, 0:16, :], src[2 * c + 1, 0:16, :]], axis=1))

    def use(c):
        x = jnp.concatenate([src[2 * c, 16:32, :], src[2 * c + 1, 16:32, :]], axis=1)
        g = gbuf[...]
        acc[...] += jnp.dot(x, g, preferred_element_type=F32)
        back = lax.dot_general(xt[...], g, over_lanes, preferred_element_type=F32).astype(BF16)
        rsr_out[2 * c] = back[:, 0:SH]
        rsr_out[2 * c + 1] = back[:, SH:2 * SH]

    def wait_chunk(c):
        @pl.when(c != own // 2)
        def _():
            arrived(2 * c, src, src_rs)

        arrived(2 * c + 1, src, src_rs)

    def images_chunk(c):
        @pl.when(c + 1 < chunks)
        def _():
            wait_chunk(c + 1)

        b = feat_b[...]
        use(c - 1)
        gbuf[...] = tile(b)
        feat_b[...] = source_features(jnp.minimum(c + 1, chunks - 1))
        for k in two_way:
            @pl.when(c - 1 == k // 2)
            def _():
                row_copy(order[k], k, rsr_out.at[k], rsr_in.at[k], rsr_ss, rsr_rs).start()

    wait_chunk(0)
    wait_chunk(1)
    gbuf[...] = tile(source_features(0))
    feat_b[...] = source_features(1)
    each(1, nc, lambda k: arrived(k, tgx, tgx_rs))
    for k in range(nc):
        xt[:, k * SH:(k + 1) * SH] = tgx[k]
    each(1, chunks, images_chunk)
    use(chunks - 1)

    def rs_send(k):
        rs_out[k] = acc[:, pl.ds(pl.multiple_of(k * SH, SH), SH)].astype(BF16)
        pltpu.make_async_remote_copy(
            src_ref=rs_out.at[k], dst_ref=rs_in.at[k], send_sem=rs_ss.at[k], recv_sem=rs_rs.at[k],
            device_id=(i, lax.rem(j + nc - k, nc)), device_id_type=MESH,
        ).start()

    each(1, nc, rs_send)

    each(0, nr - 1, lambda k: arrived(k, fpk, fpk_rs))
    packets = fpk[...].reshape(nr, 128)
    quarter = lax.broadcasted_iota(jnp.int32, (nz, 128), 1) // FD
    comps = []
    for c in range(4):
        comp = jnp.zeros((nz, 128), F32)
        for a in range(ny):
            moved = packets[a * nz:(a + 1) * nz]
            if a != c:
                moved = pltpu.roll(moved, FD * (a - c) % 128, 1)
            comp = jnp.where(quarter == a, moved, comp)
        comps.append(comp)
    frows = pieces([comp * CYCLES for comp in comps[:3]])
    detectors = lax.broadcasted_iota(jnp.int32, (GROUPS, 128), 0).astype(F32)
    for m in range(nz):
        for n, part in enumerate(frows):
            fgeo[m, n:n + 1, :] = part[m:m + 1]
        fgeo[m, 13:16, :] = jnp.zeros((3, 128), F32)
        onehot[:, m * 128:(m + 1) * 128] = (detectors == comps[3][m:m + 1]).astype(BF16)

    for c in range(nz // 2):
        feat_f[c * 256:(c + 1) * 256, :] = features_b(
            jnp.concatenate([fgeo[2 * c], fgeo[2 * c + 1]], axis=1).astype(BF16))

    def field_chunk(c):
        g = tile(feat_f[pl.ds(pl.multiple_of(c * 256, 256), 256), :])
        for q in range(nc // 2):
            gf[q, pl.ds(pl.multiple_of(c * 256, 256), 256), :] = g[:, q * 256:(q + 1) * 256]

    early = nz // 4
    each(0, early, field_chunk)

    rs_in[0] = jnp.zeros((WV, SH), BF16)
    total = acc[:, 0:SH]
    each(1, nc, lambda k: arrived(k, rs_in, rs_rs))
    total = total + jnp.sum(rs_in[...].astype(F32), axis=0)
    for k in two_way:
        arrived(k, rsr_in, rsr_rs)
        total = total + rsr_in[k].astype(F32)
    residual = inc[...] - self_term[...] * start - total * scale
    density = start + damping * precondition(residual)
    den_o[...] = density
    den[0] = (density * weight[...]).astype(BF16)
    each(1, nc, lambda k: col_copy(k, den.at[0], den.at[k], den_ss, den_rs).start())

    each(early, nz // 2, field_chunk)
    facc[...] = jnp.zeros_like(facc)

    def field_sum(q):
        @pl.when(q > 0)
        def _():
            arrived(2 * q, den, den_rs)

        arrived(2 * q + 1, den, den_rs)
        x = jnp.concatenate([den[2 * q], den[2 * q + 1]], axis=1)
        facc[...] += lax.dot_general(x, gf[q], over_lanes, preferred_element_type=F32)

    each(0, nc // 2, field_sum)

    fsum = facc[...] * scale
    h, m, l = split3(fsum)
    parts = jnp.concatenate([h.astype(BF16), m.astype(BF16), l.astype(BF16)], axis=0)
    sums = lax.dot_general(parts, onehot[...], over_lanes, preferred_element_type=F32)
    detp[...] = sums[0:WV] + sums[WV:2 * WV] + sums[2 * WV:3 * WV]

    def waves_of(col):
        return pl.ds(pl.multiple_of(lax.rem(col, 2) * 8, 8), 8)

    each(1, nc, lambda k: col_copy(k, detp.at[waves_of(j + k)], det1.at[j], d1_ss, d1_rs).start())
    det1[j] = detp[waves_of(j), :]

    for m in range(nz):
        pot_out[m] = fsum[:, m * 128:(m + 1) * 128].astype(BF16)
    for k, d in enumerate(others):
        row_copy(d, k, pot_out.at[lax.rem(iz + d[0], nz)], pot_in.at[k], pot_ss, pot_rs).start()

    each(1, nc, lambda k: arrived(k, det1, d1_rs))
    det2[i] = jnp.sum(det1[...], axis=0)
    for k, d in enumerate(others):
        row_copy(d, k, det2.at[i], det2.at[i], d2_ss, d2_rs).start()

    each(0, nr - 1, lambda k: arrived(k, pot_in, pot_rs))
    pot_in[nr - 1] = pot_out[iz]
    pot = jnp.sum(pot_in[...].astype(F32), axis=0)
    pot = pltpu.roll(pot, lax.rem(128 - FD * iy, 128), 1)
    pot_o[...] = pot[:, 0:FD].astype(BF16)

    each(0, nr - 1, lambda k: arrived(k, det2, d2_rs))
    core = lax.rem(j, 2)
    det3[core] = jnp.sum(det2[...], axis=0) * wave_scale
    swap = pltpu.make_async_remote_copy(
        src_ref=det3.at[core], dst_ref=det3.at[core], send_sem=d3_s.at[0], recv_sem=d3_s.at[1],
        device_id=(i, j + 1 - 2 * core), device_id_type=MESH,
    )
    swap.start()
    swap.wait()
    det_o[...] = jnp.concatenate([det3[0], det3[1]], axis=0)

    def sent(ks, buf, ss):
        def wait(k):
            pltpu.make_async_remote_copy(
                src_ref=buf.at[0], dst_ref=buf.at[0], send_sem=ss.at[k], recv_sem=ss.at[k],
                device_id=(i, j), device_id_type=MESH,
            ).wait_send()

        if isinstance(ks, range):
            each(ks.start, ks.stop, wait)
        else:
            for k in ks:
                wait(k)

    sent(range(1, nc), tgt, tgt_ss)
    sent(range(1, nc), tgx, tgx_ss)
    sent(range(0, own), src, src_ss)
    sent(range(own + 1, len(order)), src, src_ss)
    sent(range(0, nr - 1), fpk, fpk_ss)
    sent(two_way, rsr_out, rsr_ss)
    sent(range(1, nc), rs_out, rs_ss)
    sent(range(1, nc), den, den_ss)
    sent(range(0, nr - 1), pot_out, pot_ss)
    sent(range(1, nc), det1, d1_ss)
    sent(range(0, nr - 1), det2, d2_ss)


def plan(nz, ny):
    def hops(d):
        return min(d[0], nz - d[0]) + 2 * min(d[1], ny - d[1])

    both = [(dz, dy) for dy in range(1, ny // 2) for dz in range(nz)]
    both += [(dz, dy) for dy in (0, ny // 2) for dz in range(1, nz // 2)]
    both = sorted(both, key=hops)
    pairs = [both[n:n + 2] for n in range(0, len(both), 2)]
    near = pairs[:len(pairs) // 2]
    far = pairs[len(pairs) // 2:][::-1]
    home = [(0, 0), (0, ny // 2)]
    last = [(nz // 2, 0), (nz // 2, ny // 2)]
    seq = near[:1] + [home] + near[1:] + far + [last]
    order = [d for pair in seq for d in pair]
    two_way = [k for k, d in enumerate(order) if d in both]
    return order, two_way, order.index((0, 0))


def local(
    nz, ny, nc, panel_xyz, panel_weight, self_term, panel_slot, block_inverse, incident, field_xyz, field_group
):
    nr = nz * ny
    panels = SH * nr * nc
    fields = field_xyz.shape[1]
    mine = nz * 128
    scale = CYCLES * LEAD / math.sqrt(panels)
    wave_scale = 1.0 / math.sqrt(fields * nr / GROUPS)
    sel_b, sel_a = selectors()
    slots = len(plan(nz, ny)[0])
    vmem, dma = pltpu.VMEM, pltpu.SemaphoreType.DMA
    sems = [dma((10,))]
    for n in (slots, nc, nc, slots, nc, nc, nr, nr, nc, nr):
        sems += [dma((n,)), dma((n,))]
    sems += [dma((2,))]
    args = (
        panel_xyz, panel_weight, self_term.reshape(1, SH), panel_slot.reshape(1, SH), block_inverse, incident,
        field_xyz, field_group.reshape(1, FD), jnp.asarray(sel_b, BF16), jnp.asarray(sel_a, BF16),
    )
    return pl.pallas_call(
        functools.partial(kernel, nz, ny, nc, scale, wave_scale),
        out_shape=(
            jax.ShapeDtypeStruct((WV, SH), F32),
            jax.ShapeDtypeStruct((WV, FD), BF16),
            jax.ShapeDtypeStruct((WV, GROUPS), F32),
        ),
        in_specs=[pl.BlockSpec(memory_space=pltpu.HBM)] * 10,
        out_specs=(pl.BlockSpec(memory_space=pltpu.VMEM),) * 3,
        scratch_shapes=[vmem(a.shape, a.dtype) for a in args] + [
            vmem((16, SH), F32),
            vmem((2, 8, 128), F32),
            vmem((slots, 32, SH), BF16),
            vmem((nc, 16, SH), BF16),
            vmem((nc, WV, SH), BF16),
            vmem((32, nc * SH), BF16),
            vmem((2 * SH, 32), BF16),
            vmem((mine, 32), BF16),
            vmem((WV, nc * SH), BF16),
            vmem((SH, SH), F32),
            vmem((WV, nc * SH), F32),
            vmem((2 * SH, nc * SH), BF16),
            vmem((slots, WV, SH), BF16),
            vmem((slots, WV, SH), BF16),
            vmem((nc, WV, SH), BF16),
            vmem((nc, WV, SH), BF16),
            vmem((nr, 1, 128), F32),
            vmem((nz, 16, 128), F32),
            vmem((GROUPS, mine), BF16),
            vmem((nc, WV, SH), BF16),
            vmem((nc // 2, mine, 256), BF16),
            vmem((WV, mine), F32),
            vmem((nz, WV, 128), BF16),
            vmem((nr, WV, 128), BF16),
            vmem((WV, GROUPS), F32),
            vmem((nc, 8, GROUPS), F32),
            vmem((nr, 8, GROUPS), F32),
            vmem((2, 8, GROUPS), F32),
        ] + sems,
        compiler_params=pltpu.CompilerParams(
            collective_id=0, has_side_effects=True, vmem_limit_bytes=67043328
        ),
    )(*args)


def solution(mesh):
    nr, nc = mesh.shape["row"], mesh.shape["col"]
    ny = 4
    return jax.shard_map(
        functools.partial(local, nr // ny, ny, nc),
        mesh=mesh,
        in_specs=(
            P(None, ("col", "row")),
            P(None, ("col", "row")),
            P(("col", "row")),
            P(("col", "row")),
            P(None, ("col", "row")),
            P(None, ("col", "row")),
            P(None, "row"),
            P(("row", "col")),
        ),
        out_specs=(P(None, ("col", "row")), P(None, ("row", "col")), P()),
        check_vma=False,
    )
```

```python
import functools
import math

import jax
import jax.numpy as jnp
import numpy as np
from jax import lax
from jax.experimental import pallas as pl
from jax.experimental.pallas import tpu as pltpu
from jax.sharding import PartitionSpec as P

MESH = pl.DeviceIdType.MESH
HIGHEST = lax.Precision.HIGHEST
F32 = jnp.float32
BF16 = jnp.bfloat16

GROUPS = 128
SH = 128
WV = 16
FD = 32
wave_number = 12.0
smoothing = 0.05
damping = 0.5

LEAD, A1, A0 = 73.90290388562806, -0.5546875, 0.0849609375
CYCLES = wave_number / (2.0 * math.pi)
EPS = smoothing * smoothing * CYCLES * CYCLES


def selectors():
    sel_b = np.zeros((16, 32), np.float32)
    sel_a = np.zeros((32, 16), np.float32)
    high, mid, low = 0, 1, 2
    pairs = [(high, high), (high, mid), (mid, high), (mid, mid), (high, low), (low, high), (mid, low), (low, mid)]
    k = 0
    for b, a in pairs:
        for c in range(3):
            sel_b[3 * b + c, k] = -2.0
            sel_a[k, 3 * a + c] = 1.0
            k += 1
    for n in range(3):
        sel_b[9 + n, k] = 1.0
        sel_a[k, 12] = 1.0
        k += 1
    for n in range(3):
        sel_b[12, k] = 1.0
        sel_a[k, 9 + n] = 1.0
        k += 1
    return sel_b, sel_a


def split3(x):
    h = x.astype(BF16).astype(F32)
    m = (x - h).astype(BF16).astype(F32)
    return h, m, (x - h) - m


def pieces(coords):
    parts = [split3(c) for c in coords]
    norm = split3(coords[0] * coords[0] + coords[1] * coords[1] + coords[2] * coords[2])
    rows = [parts[c][p] for p in range(3) for c in range(3)]
    return rows + list(norm) + [jnp.ones_like(norm[0])]


def pair_values(d):
    s = jnp.maximum(d, 1e-12)
    r = s * lax.rsqrt(s)
    v = (0.25 - jnp.abs(r - jnp.round(r))).astype(BF16)
    q = v * v
    p = (q + BF16(A1)) * q + BF16(A0)
    return (p * v) * lax.rsqrt(s + EPS).astype(BF16)


def kernel(
    nz, ny, nc, scale, wave_scale,
    xyz_h, weight_h, self_h, slot_h, binv_h, inc_h, fxyz_h, fgroup_h, sel_b_h, sel_a_h,
    den_o, pot_o, det_o,
    xyz, weight, self_term, slot, binv, inc, fxyz, fgroup, sel_b, sel_a,
    geo_s, fs, src, tgt, tgx, feat_a, feat_b, feat_f, xt, coupled, acc, gbuf, rsr_out, rsr_in, rs_out, rs_in, fpk, fgeo, onehot,
    den, gf, pot_out, pot_in, detp, det1, det2, det3,
    load_s, src_ss, src_rs, tgt_ss, tgt_rs, tgx_ss, tgx_rs, rsr_ss, rsr_rs, rs_ss, rs_rs, den_ss, den_rs, fpk_ss, fpk_rs,
    pot_ss, pot_rs, d1_ss, d1_rs, d2_ss, d2_rs, d3_s,
):
    nr = nz * ny
    i = lax.axis_index("row")
    j = lax.axis_index("col")
    iz, iy = i // ny, i % ny
    order, two_way, own = plan(nz, ny)
    chunks = len(order) // 2

    def each(lo, hi, body):
        def step(n, _):
            body(n)
            return 0

        lax.fori_loop(lo, hi, step, 0)

    barrier = pltpu.get_barrier_semaphore()
    each(0, nr - 1, lambda n: pl.semaphore_signal(
        barrier, inc=1, device_id=(lax.rem(i + 1 + lax.rem(n + nr // 2 - 1, nr - 1), nr), j), device_id_type=MESH))
    each(1, nc, lambda n: pl.semaphore_signal(
        barrier, inc=1, device_id=(i, lax.rem(j + n, nc)), device_id_type=MESH))

    loads = [
        pltpu.make_async_copy(a, b, load_s.at[n])
        for n, (a, b) in enumerate([
            (xyz_h, xyz), (weight_h, weight), (self_h, self_term), (slot_h, slot), (binv_h, binv), (inc_h, inc),
            (fxyz_h, fxyz), (fgroup_h, fgroup), (sel_b_h, sel_b), (sel_a_h, sel_a),
        ])
    ]
    for load in loads:
        load.start()
    for load in loads:
        load.wait()

    rows = pieces([xyz[c:c + 1, :] * CYCLES for c in range(3)])
    for n, row in enumerate(rows):
        geo_s[n:n + 1, :] = row
    geo_s[13:16, :] = jnp.zeros((3, SH), F32)
    packet = geo_s[...].astype(BF16)
    src[own, 0:16, :] = packet
    tgt[0] = packet
    place = lax.broadcasted_iota(jnp.int32, (64, SH), 0)
    chosen = (place == slot[...] % 64).astype(F32)
    half = (lax.broadcasted_iota(jnp.int32, (8, SH), 0) == slot[...] // 64).astype(F32)
    over_rows = (((0,), (0,)), ((), ()))
    over_lanes = (((1,), (1,)), ((), ()))
    picked = lax.dot_general(binv[...], chosen, over_rows, precision=HIGHEST, preferred_element_type=F32)
    same = lax.dot_general(half, half, over_rows, preferred_element_type=F32)
    coupled[...] = picked * same

    def precondition(values):
        mixing = jnp.dot(values, coupled[...], precision=HIGHEST, preferred_element_type=F32)
        return values / self_term[...] + mixing

    start = precondition(inc[...])
    start_w = (start * weight[...]).astype(BF16)
    src[own, 16:32, :] = start_w
    tgx[0] = start_w

    lane = lax.broadcasted_iota(jnp.int32, (8, 128), 1)
    fs[...] = jnp.zeros_like(fs)
    fs[0, 0:3, :] = fxyz[:, pl.ds(pl.multiple_of(j // 4 * 128, 128), 128)]
    fs[1, 0:1, 0:FD] = fgroup[...].astype(F32)
    points = pltpu.roll(fs[0], lax.rem(128 - FD * lax.rem(j, 4), 128), 1)
    points = jnp.where(lane < FD, points, 0.0)
    row = points[0:1] + pltpu.roll(points, FD, 1)[1:2] + pltpu.roll(points, 2 * FD, 1)[2:3]
    row = row + pltpu.roll(fs[1], 3 * FD, 1)[0:1]
    mine = iy * nz + iz
    fpk[mine] = row

    pl.semaphore_wait(barrier, nr + nc - 2)

    def row_copy(d, k, src_ref, dst_ref, ss, rs):
        dz, dy = d
        peer = lax.rem(iz + dz % nz, nz) * ny + lax.rem(iy + dy % ny, ny)
        return pltpu.make_async_remote_copy(
            src_ref=src_ref, dst_ref=dst_ref, send_sem=ss.at[k], recv_sem=rs.at[k],
            device_id=(peer, j), device_id_type=MESH,
        )

    def col_copy(k, src_ref, dst_ref, ss, rs):
        return pltpu.make_async_remote_copy(
            src_ref=src_ref, dst_ref=dst_ref, send_sem=ss.at[k], recv_sem=rs.at[k],
            device_id=(i, lax.rem(j + k, nc)), device_id_type=MESH,
        )

    def arrived(k, buf, rs):
        pltpu.make_async_remote_copy(
            src_ref=buf.at[0], dst_ref=buf.at[0], send_sem=rs.at[k], recv_sem=rs.at[k],
            device_id=(i, j), device_id_type=MESH,
        ).wait_recv()

    each(1, nc, lambda k: col_copy(k, tgt.at[0], tgt.at[k], tgt_ss, tgt_rs).start())
    for k, (dz, dy) in enumerate(order):
        if k == 4:
            each(1, nc, lambda n: col_copy(n, tgx.at[0], tgx.at[n], tgx_ss, tgx_rs).start())
        if k != own:
            row_copy((-dz, -dy), k, src.at[own], src.at[k], src_ss, src_rs).start()
    others = sorted([(dz, dy) for dz in range(nz) for dy in range(ny)][1:],
                    key=lambda d: -min(d[0], nz - d[0]) - 2 * min(d[1], ny - d[1]))
    for k, d in enumerate(others):
        row_copy(d, k, fpk.at[mine], fpk.at[mine], fpk_ss, fpk_rs).start()

    def features_a(pk):
        return jnp.dot(sel_a[...], pk, preferred_element_type=F32).astype(BF16)

    def features_b(pk):
        return lax.dot_general(pk, sel_b[...], over_rows, preferred_element_type=F32).astype(BF16)

    acc[...] = jnp.zeros_like(acc)

    each(1, nc, lambda k: arrived(k, tgt, tgt_rs))
    for k in range(0, nc, 4):
        feat_a[:, k * SH:(k + 4) * SH] = features_a(jnp.concatenate([tgt[n] for n in range(k, k + 4)], axis=1))

    def tile(b):
        return pair_values(jnp.dot(b, feat_a[...], preferred_element_type=F32))

    def source_features(c):
        return features_b(jnp.concatenate([src[2 * c, 0:16, :], src[2 * c + 1, 0:16, :]], axis=1))

    def use(c):
        x = jnp.concatenate([src[2 * c, 16:32, :], src[2 * c + 1, 16:32, :]], axis=1)
        g = gbuf[...]
        acc[...] += jnp.dot(x, g, preferred_element_type=F32)
        back = lax.dot_general(xt[...], g, over_lanes, preferred_element_type=F32).astype(BF16)
        rsr_out[2 * c] = back[:, 0:SH]
        rsr_out[2 * c + 1] = back[:, SH:2 * SH]

    def wait_chunk(c):
        @pl.when(c != own // 2)
        def _():
            arrived(2 * c, src, src_rs)

        arrived(2 * c + 1, src, src_rs)

    def images_chunk(c):
        @pl.when(c + 1 < chunks)
        def _():
            wait_chunk(c + 1)

        b = feat_b[...]
        use(c - 1)
        gbuf[...] = tile(b)
        feat_b[...] = source_features(jnp.minimum(c + 1, chunks - 1))
        for k in two_way:
            @pl.when(c - 1 == k // 2)
            def _():
                row_copy(order[k], k, rsr_out.at[k], rsr_in.at[k], rsr_ss, rsr_rs).start()

    wait_chunk(0)
    wait_chunk(1)
    gbuf[...] = tile(source_features(0))
    feat_b[...] = source_features(1)
    each(1, nc, lambda k: arrived(k, tgx, tgx_rs))
    for k in range(nc):
        xt[:, k * SH:(k + 1) * SH] = tgx[k]
    each(1, chunks, images_chunk)
    use(chunks - 1)

    def rs_send(k):
        rs_out[k] = acc[:, pl.ds(pl.multiple_of(k * SH, SH), SH)].astype(BF16)
        pltpu.make_async_remote_copy(
            src_ref=rs_out.at[k], dst_ref=rs_in.at[k], send_sem=rs_ss.at[k], recv_sem=rs_rs.at[k],
            device_id=(i, lax.rem(j + nc - k, nc)), device_id_type=MESH,
        ).start()

    each(1, nc, rs_send)

    each(0, nr - 1, lambda k: arrived(k, fpk, fpk_rs))
    packets = fpk[...].reshape(nr, 128)
    quarter = lax.broadcasted_iota(jnp.int32, (nz, 128), 1) // FD
    comps = []
    for c in range(4):
        comp = jnp.zeros((nz, 128), F32)
        for a in range(ny):
            moved = packets[a * nz:(a + 1) * nz]
            if a != c:
                moved = pltpu.roll(moved, FD * (a - c) % 128, 1)
            comp = jnp.where(quarter == a, moved, comp)
        comps.append(comp)
    frows = pieces([comp * CYCLES for comp in comps[:3]])
    detectors = lax.broadcasted_iota(jnp.int32, (GROUPS, 128), 0).astype(F32)
    for m in range(nz):
        for n, part in enumerate(frows):
            fgeo[m, n:n + 1, :] = part[m:m + 1]
        fgeo[m, 13:16, :] = jnp.zeros((3, 128), F32)
        onehot[:, m * 128:(m + 1) * 128] = (detectors == comps[3][m:m + 1]).astype(BF16)

    for c in range(nz // 2):
        feat_f[c * 256:(c + 1) * 256, :] = features_b(
            jnp.concatenate([fgeo[2 * c], fgeo[2 * c + 1]], axis=1).astype(BF16))

    def field_chunk(c):
        g = tile(feat_f[pl.ds(pl.multiple_of(c * 256, 256), 256), :])
        gf[pl.ds(pl.multiple_of(c * 256, 256), 256), :] = g

    early = nz // 4
    each(0, early, field_chunk)

    rs_in[0] = jnp.zeros((WV, SH), BF16)
    total = acc[:, 0:SH]
    each(1, nc, lambda k: arrived(k, rs_in, rs_rs))
    total = total + jnp.sum(rs_in[...].astype(F32), axis=0)
    for k in two_way:
        arrived(k, rsr_in, rsr_rs)
        total = total + rsr_in[k].astype(F32)
    residual = inc[...] - self_term[...] * start - total * scale
    density = start + damping * precondition(residual)
    den_o[...] = density
    den[0] = (density * weight[...]).astype(BF16)
    each(1, nc, lambda k: col_copy(k, den.at[0], den.at[k], den_ss, den_rs).start())

    each(early, nz // 2, field_chunk)
    each(1, nc, lambda k: arrived(k, den, den_rs))
    x = jnp.concatenate([den[k] for k in range(nc)], axis=1)
    fsum = lax.dot_general(x, gf[...], over_lanes, preferred_element_type=F32) * scale
    h, m, l = split3(fsum)
    parts = jnp.concatenate([h.astype(BF16), m.astype(BF16), l.astype(BF16)], axis=0)
    sums = lax.dot_general(parts, onehot[...], over_lanes, preferred_element_type=F32)
    detp[...] = sums[0:WV] + sums[WV:2 * WV] + sums[2 * WV:3 * WV]

    def waves_of(col):
        return pl.ds(pl.multiple_of(lax.rem(col, 2) * 8, 8), 8)

    each(1, nc, lambda k: col_copy(k, detp.at[waves_of(j + k)], det1.at[j], d1_ss, d1_rs).start())
    det1[j] = detp[waves_of(j), :]

    for m in range(nz):
        pot_out[m] = fsum[:, m * 128:(m + 1) * 128].astype(BF16)
    for k, d in enumerate(others):
        row_copy(d, k, pot_out.at[lax.rem(iz + d[0], nz)], pot_in.at[k], pot_ss, pot_rs).start()

    each(1, nc, lambda k: arrived(k, det1, d1_rs))
    det2[i] = jnp.sum(det1[...], axis=0)
    for k, d in enumerate(others):
        row_copy(d, k, det2.at[i], det2.at[i], d2_ss, d2_rs).start()

    each(0, nr - 1, lambda k: arrived(k, pot_in, pot_rs))
    pot_in[nr - 1] = pot_out[iz]
    pot = jnp.sum(pot_in[...].astype(F32), axis=0)
    pot = pltpu.roll(pot, lax.rem(128 - FD * iy, 128), 1)
    pot_o[...] = pot[:, 0:FD].astype(BF16)

    each(0, nr - 1, lambda k: arrived(k, det2, d2_rs))
    core = lax.rem(j, 2)
    det3[core] = jnp.sum(det2[...], axis=0) * wave_scale
    swap = pltpu.make_async_remote_copy(
        src_ref=det3.at[core], dst_ref=det3.at[core], send_sem=d3_s.at[0], recv_sem=d3_s.at[1],
        device_id=(i, j + 1 - 2 * core), device_id_type=MESH,
    )
    swap.start()
    swap.wait()
    det_o[...] = jnp.concatenate([det3[0], det3[1]], axis=0)

    def sent(ks, buf, ss):
        def wait(k):
            pltpu.make_async_remote_copy(
                src_ref=buf.at[0], dst_ref=buf.at[0], send_sem=ss.at[k], recv_sem=ss.at[k],
                device_id=(i, j), device_id_type=MESH,
            ).wait_send()

        if isinstance(ks, range):
            each(ks.start, ks.stop, wait)
        else:
            for k in ks:
                wait(k)

    sent(range(1, nc), tgt, tgt_ss)
    sent(range(1, nc), tgx, tgx_ss)
    sent(range(0, own), src, src_ss)
    sent(range(own + 1, len(order)), src, src_ss)
    sent(range(0, nr - 1), fpk, fpk_ss)
    sent(two_way, rsr_out, rsr_ss)
    sent(range(1, nc), rs_out, rs_ss)
    sent(range(1, nc), den, den_ss)
    sent(range(0, nr - 1), pot_out, pot_ss)
    sent(range(1, nc), det1, d1_ss)
    sent(range(0, nr - 1), det2, d2_ss)


def plan(nz, ny):
    def hops(d):
        return min(d[0], nz - d[0]) + 2 * min(d[1], ny - d[1])

    both = [(dz, dy) for dy in range(1, ny // 2) for dz in range(nz)]
    both += [(dz, dy) for dy in (0, ny // 2) for dz in range(1, nz // 2)]
    both = sorted(both, key=hops)
    pairs = [both[n:n + 2] for n in range(0, len(both), 2)]
    near = pairs[:len(pairs) // 2]
    far = pairs[len(pairs) // 2:][::-1]
    home = [(0, 0), (0, ny // 2)]
    last = [(nz // 2, 0), (nz // 2, ny // 2)]
    seq = near[:1] + [home] + near[1:] + far + [last]
    order = [d for pair in seq for d in pair]
    two_way = [k for k, d in enumerate(order) if d in both]
    return order, two_way, order.index((0, 0))


def local(
    nz, ny, nc, panel_xyz, panel_weight, self_term, panel_slot, block_inverse, incident, field_xyz, field_group
):
    nr = nz * ny
    panels = SH * nr * nc
    fields = field_xyz.shape[1]
    mine = nz * 128
    scale = CYCLES * LEAD / math.sqrt(panels)
    wave_scale = 1.0 / math.sqrt(fields * nr / GROUPS)
    sel_b, sel_a = selectors()
    slots = len(plan(nz, ny)[0])
    vmem, dma = pltpu.VMEM, pltpu.SemaphoreType.DMA
    sems = [dma((10,))]
    for n in (slots, nc, nc, slots, nc, nc, nr, nr, nc, nr):
        sems += [dma((n,)), dma((n,))]
    sems += [dma((2,))]
    args = (
        panel_xyz, panel_weight, self_term.reshape(1, SH), panel_slot.reshape(1, SH), block_inverse, incident,
        field_xyz, field_group.reshape(1, FD), jnp.asarray(sel_b, BF16), jnp.asarray(sel_a, BF16),
    )
    shapes = (
        jax.ShapeDtypeStruct((WV, SH), F32),
        jax.ShapeDtypeStruct((WV, FD), BF16),
        jax.ShapeDtypeStruct((WV, GROUPS), F32),
    )
    hbm = pl.BlockSpec(memory_space=pltpu.HBM)
    results = pl.pallas_call(
        functools.partial(kernel, nz, ny, nc, scale, wave_scale),
        out_shape=shapes,
        in_specs=[pl.BlockSpec(memory_space=pltpu.HBM)] * 10,
        out_specs=(pl.BlockSpec(memory_space=pltpu.VMEM),) * 3,
        scratch_shapes=[vmem(a.shape, a.dtype) for a in args] + [
            vmem((16, SH), F32),
            vmem((2, 8, 128), F32),
            vmem((slots, 32, SH), BF16),
            vmem((nc, 16, SH), BF16),
            vmem((nc, WV, SH), BF16),
            vmem((32, nc * SH), BF16),
            vmem((2 * SH, 32), BF16),
            vmem((mine, 32), BF16),
            vmem((WV, nc * SH), BF16),
            vmem((SH, SH), F32),
            vmem((WV, nc * SH), F32),
            vmem((2 * SH, nc * SH), BF16),
            vmem((slots, WV, SH), BF16),
            vmem((slots, WV, SH), BF16),
            vmem((nc, WV, SH), BF16),
            vmem((nc, WV, SH), BF16),
            vmem((nr, 1, 128), F32),
            vmem((nz, 16, 128), F32),
            vmem((GROUPS, mine), BF16),
            vmem((nc, WV, SH), BF16),
            vmem((mine, nc * SH), BF16),
            vmem((nz, WV, 128), BF16),
            vmem((nr, WV, 128), BF16),
            vmem((WV, GROUPS), F32),
            vmem((nc, 8, GROUPS), F32),
            vmem((nr, 8, GROUPS), F32),
            vmem((2, 8, GROUPS), F32),
        ] + sems,
        compiler_params=pltpu.CompilerParams(
            collective_id=0, has_side_effects=True, vmem_limit_bytes=67043328
        ),
    )(*args)
    return pl.pallas_call(
        hand_out,
        out_shape=shapes,
        in_specs=[hbm] * 3,
        out_specs=(hbm,) * 3,
        scratch_shapes=[vmem(a.shape, a.dtype) for a in shapes] + [dma((3,)), dma((3,))],
        compiler_params=pltpu.CompilerParams(vmem_limit_bytes=67043328),
    )(*results)


def hand_out(a0, a1, a2, o0, o1, o2, s0, s1, s2, in_s, out_s):
    taken = [pltpu.make_async_copy(a, s, in_s.at[n]) for n, (a, s) in enumerate(((a0, s0), (a1, s1), (a2, s2)))]
    given = [pltpu.make_async_copy(s, o, out_s.at[n]) for n, (s, o) in enumerate(((s0, o0), (s1, o1), (s2, o2)))]
    for copy in taken:
        copy.start()
    for copy, put in zip(taken, given):
        copy.wait()
        put.start()
    for put in given:
        put.wait()


def solution(mesh):
    nr, nc = mesh.shape["row"], mesh.shape["col"]
    ny = 4
    return jax.shard_map(
        functools.partial(local, nr // ny, ny, nc),
        mesh=mesh,
        in_specs=(
            P(None, ("col", "row")),
            P(None, ("col", "row")),
            P(("col", "row")),
            P(("col", "row")),
            P(None, ("col", "row")),
            P(None, ("col", "row")),
            P(None, "row"),
            P(("row", "col")),
        ),
        out_specs=(P(None, ("col", "row")), P(None, ("row", "col")), P()),
        check_vma=False,
    )
```

```python
import functools
import math

import jax
import jax.numpy as jnp
import numpy as np
from jax import lax
from jax.experimental import pallas as pl
from jax.experimental.pallas import tpu as pltpu
from jax.sharding import PartitionSpec as P

MESH = pl.DeviceIdType.MESH
HIGHEST = lax.Precision.HIGHEST
F32 = jnp.float32
BF16 = jnp.bfloat16

GROUPS = 128
SH = 128
WV = 16
FD = 32
wave_number = 12.0
smoothing = 0.05
damping = 0.5

LEAD, A1, A0 = 73.90290388562806, -0.5546875, 0.0849609375
CYCLES = wave_number / (2.0 * math.pi)
EPS = smoothing * smoothing * CYCLES * CYCLES


def selectors():
    sel_b = np.zeros((16, 32), np.float32)
    sel_a = np.zeros((32, 16), np.float32)
    high, mid, low = 0, 1, 2
    pairs = [(high, high), (high, mid), (mid, high), (mid, mid), (high, low), (low, high), (mid, low), (low, mid)]
    k = 0
    for b, a in pairs:
        for c in range(3):
            sel_b[3 * b + c, k] = -2.0
            sel_a[k, 3 * a + c] = 1.0
            k += 1
    for n in range(3):
        sel_b[9 + n, k] = 1.0
        sel_a[k, 12] = 1.0
        k += 1
    for n in range(3):
        sel_b[12, k] = 1.0
        sel_a[k, 9 + n] = 1.0
        k += 1
    return sel_b, sel_a


def split3(x):
    h = x.astype(BF16).astype(F32)
    m = (x - h).astype(BF16).astype(F32)
    return h, m, (x - h) - m


def pieces(coords):
    parts = [split3(c) for c in coords]
    norm = split3(coords[0] * coords[0] + coords[1] * coords[1] + coords[2] * coords[2])
    rows = [parts[c][p] for p in range(3) for c in range(3)]
    return rows + list(norm) + [jnp.ones_like(norm[0])]


def pair_values(d):
    s = jnp.maximum(d, 1e-12)
    r = s * lax.rsqrt(s)
    v = (0.25 - jnp.abs(r - jnp.round(r))).astype(BF16)
    q = v * v
    p = (q + BF16(A1)) * q + BF16(A0)
    return (p * v) * lax.rsqrt(s + EPS).astype(BF16)


def kernel(
    nz, ny, nc, scale, wave_scale,
    xyz_h, weight_h, self_h, slot_h, binv_h, inc_h, fxyz_h, fgroup_h, sel_b_h, sel_a_h,
    den_o, pot_o, det_o,
    xyz, weight, self_term, slot, binv, inc, fxyz, fgroup, sel_b, sel_a,
    geo_s, fs, src, tgt, tgx, feat_a, feat_b, feat_f, xt, coupled, acc, gbuf, rsr_out, rsr_in, rs_out, rs_in, fpk, fgeo, onehot,
    den, gf, pot_out, pot_in, detp, det1, det2, detz, det3,
    load_s, src_ss, src_rs, tgt_ss, tgt_rs, tgx_ss, tgx_rs, rsr_ss, rsr_rs, rs_ss, rs_rs, den_ss, den_rs, fpk_ss, fpk_rs,
    pot_ss, pot_rs, d1_ss, d1_rs, d2_ss, d2_rs, d3_s,
):
    nr = nz * ny
    i = lax.axis_index("row")
    j = lax.axis_index("col")
    iz, iy = i // ny, i % ny
    order, two_way, own = plan(nz, ny)
    chunks = len(order) // 2

    def each(lo, hi, body):
        def step(n, _):
            body(n)
            return 0

        lax.fori_loop(lo, hi, step, 0)

    barrier = pltpu.get_barrier_semaphore()
    each(0, nr - 1, lambda n: pl.semaphore_signal(
        barrier, inc=1, device_id=(lax.rem(i + 1 + lax.rem(n + nr // 2 - 1, nr - 1), nr), j), device_id_type=MESH))
    each(1, nc, lambda n: pl.semaphore_signal(
        barrier, inc=1, device_id=(i, lax.rem(j + n, nc)), device_id_type=MESH))

    loads = [
        pltpu.make_async_copy(a, b, load_s.at[n])
        for n, (a, b) in enumerate([
            (xyz_h, xyz), (weight_h, weight), (self_h, self_term), (slot_h, slot), (binv_h, binv), (inc_h, inc),
            (fxyz_h, fxyz), (fgroup_h, fgroup), (sel_b_h, sel_b), (sel_a_h, sel_a),
        ])
    ]
    for load in loads:
        load.start()
    for load in loads:
        load.wait()

    rows = pieces([xyz[c:c + 1, :] * CYCLES for c in range(3)])
    for n, row in enumerate(rows):
        geo_s[n:n + 1, :] = row
    geo_s[13:16, :] = jnp.zeros((3, SH), F32)
    packet = geo_s[...].astype(BF16)
    src[own, 0:16, :] = packet
    tgt[0] = packet
    place = lax.broadcasted_iota(jnp.int32, (64, SH), 0)
    chosen = (place == slot[...] % 64).astype(F32)
    half = (lax.broadcasted_iota(jnp.int32, (8, SH), 0) == slot[...] // 64).astype(F32)
    over_rows = (((0,), (0,)), ((), ()))
    over_lanes = (((1,), (1,)), ((), ()))
    picked = lax.dot_general(binv[...], chosen, over_rows, precision=HIGHEST, preferred_element_type=F32)
    same = lax.dot_general(half, half, over_rows, preferred_element_type=F32)
    coupled[...] = picked * same

    def precondition(values):
        mixing = jnp.dot(values, coupled[...], precision=HIGHEST, preferred_element_type=F32)
        return values / self_term[...] + mixing

    start = precondition(inc[...])
    start_w = (start * weight[...]).astype(BF16)
    src[own, 16:32, :] = start_w
    tgx[0] = start_w

    lane = lax.broadcasted_iota(jnp.int32, (8, 128), 1)
    fs[...] = jnp.zeros_like(fs)
    fs[0, 0:3, :] = fxyz[:, pl.ds(pl.multiple_of(j // 4 * 128, 128), 128)]
    fs[1, 0:1, 0:FD] = fgroup[...].astype(F32)
    points = pltpu.roll(fs[0], lax.rem(128 - FD * lax.rem(j, 4), 128), 1)
    points = jnp.where(lane < FD, points, 0.0)
    row = points[0:1] + pltpu.roll(points, FD, 1)[1:2] + pltpu.roll(points, 2 * FD, 1)[2:3]
    row = row + pltpu.roll(fs[1], 3 * FD, 1)[0:1]
    mine = iy * nz + iz
    fpk[mine] = row

    pl.semaphore_wait(barrier, nr + nc - 2)

    def row_copy(d, k, src_ref, dst_ref, ss, rs):
        dz, dy = d
        peer = lax.rem(iz + dz % nz, nz) * ny + lax.rem(iy + dy % ny, ny)
        return pltpu.make_async_remote_copy(
            src_ref=src_ref, dst_ref=dst_ref, send_sem=ss.at[k], recv_sem=rs.at[k],
            device_id=(peer, j), device_id_type=MESH,
        )

    def col_copy(k, src_ref, dst_ref, ss, rs):
        return pltpu.make_async_remote_copy(
            src_ref=src_ref, dst_ref=dst_ref, send_sem=ss.at[k], recv_sem=rs.at[k],
            device_id=(i, lax.rem(j + k, nc)), device_id_type=MESH,
        )

    def arrived(k, buf, rs):
        pltpu.make_async_remote_copy(
            src_ref=buf.at[0], dst_ref=buf.at[0], send_sem=rs.at[k], recv_sem=rs.at[k],
            device_id=(i, j), device_id_type=MESH,
        ).wait_recv()

    each(1, nc, lambda k: col_copy(k, tgt.at[0], tgt.at[k], tgt_ss, tgt_rs).start())
    for k, (dz, dy) in enumerate(order):
        if k == 4:
            each(1, nc, lambda n: col_copy(n, tgx.at[0], tgx.at[n], tgx_ss, tgx_rs).start())
        if k != own:
            row_copy((-dz, -dy), k, src.at[own], src.at[k], src_ss, src_rs).start()
    others = sorted([(dz, dy) for dz in range(nz) for dy in range(ny)][1:],
                    key=lambda d: -min(d[0], nz - d[0]) - 2 * min(d[1], ny - d[1]))
    for k, d in enumerate(others):
        row_copy(d, k, fpk.at[mine], fpk.at[mine], fpk_ss, fpk_rs).start()

    def features_a(pk):
        return jnp.dot(sel_a[...], pk, preferred_element_type=F32).astype(BF16)

    def features_b(pk):
        return lax.dot_general(pk, sel_b[...], over_rows, preferred_element_type=F32).astype(BF16)

    acc[...] = jnp.zeros_like(acc)

    def tile(b):
        return pair_values(jnp.dot(b, feat_a[...], preferred_element_type=F32))

    def source_features(c):
        return features_b(jnp.concatenate([src[2 * c, 0:16, :], src[2 * c + 1, 0:16, :]], axis=1))

    def use(c, last=False):
        x = jnp.concatenate([src[2 * c, 16:32, :], src[2 * c + 1, 16:32, :]], axis=1)
        g = gbuf[...]
        acc[...] += jnp.dot(x, g, preferred_element_type=F32)
        if last:
            return
        back = lax.dot_general(xt[...], g, over_lanes, preferred_element_type=F32).astype(BF16)
        rsr_out[2 * c] = back[:, 0:SH]
        rsr_out[2 * c + 1] = back[:, SH:2 * SH]

    def wait_chunk(c):
        @pl.when(c != own // 2)
        def _():
            arrived(2 * c, src, src_rs)

        arrived(2 * c + 1, src, src_rs)

    def images_chunk(c):
        @pl.when(c + 1 < chunks)
        def _():
            wait_chunk(c + 1)

        b = feat_b[...]
        use(c - 1)
        gbuf[...] = tile(b)
        feat_b[...] = source_features(jnp.minimum(c + 1, chunks - 1))
        for k in two_way:
            @pl.when(c - 1 == k // 2)
            def _():
                row_copy(order[k], k, rsr_out.at[k], rsr_in.at[k], rsr_ss, rsr_rs).start()

    wait_chunk(0)
    first = source_features(0)
    wait_chunk(1)
    feat_b[...] = source_features(1)
    each(1, nc, lambda k: arrived(k, tgt, tgt_rs))
    for k in range(0, nc, 4):
        feat_a[:, k * SH:(k + 4) * SH] = features_a(jnp.concatenate([tgt[n] for n in range(k, k + 4)], axis=1))
    gbuf[...] = tile(first)
    each(1, nc, lambda k: arrived(k, tgx, tgx_rs))
    for k in range(nc):
        xt[:, k * SH:(k + 1) * SH] = tgx[k]
    each(1, chunks, images_chunk)
    use(chunks - 1, last=True)

    def rs_send(k):
        rs_out[k] = acc[:, pl.ds(pl.multiple_of(k * SH, SH), SH)].astype(BF16)
        pltpu.make_async_remote_copy(
            src_ref=rs_out.at[k], dst_ref=rs_in.at[k], send_sem=rs_ss.at[k], recv_sem=rs_rs.at[k],
            device_id=(i, lax.rem(j + nc - k, nc)), device_id_type=MESH,
        ).start()

    each(1, nc, rs_send)

    each(0, nr - 1, lambda k: arrived(k, fpk, fpk_rs))
    packets = fpk[...].reshape(nr, 128)
    quarter = lax.broadcasted_iota(jnp.int32, (nz, 128), 1) // FD
    comps = []
    for c in range(4):
        comp = jnp.zeros((nz, 128), F32)
        for a in range(ny):
            moved = packets[a * nz:(a + 1) * nz]
            if a != c:
                moved = pltpu.roll(moved, FD * (a - c) % 128, 1)
            comp = jnp.where(quarter == a, moved, comp)
        comps.append(comp)
    frows = pieces([comp * CYCLES for comp in comps[:3]])
    detectors = lax.broadcasted_iota(jnp.int32, (GROUPS, 128), 0).astype(F32)
    for m in range(nz):
        for n, part in enumerate(frows):
            fgeo[m, n:n + 1, :] = part[m:m + 1]
        fgeo[m, 13:16, :] = jnp.zeros((3, 128), F32)
        onehot[:, m * 128:(m + 1) * 128] = (detectors == comps[3][m:m + 1]).astype(BF16)

    for c in range(nz // 2):
        feat_f[c * 256:(c + 1) * 256, :] = features_b(
            jnp.concatenate([fgeo[2 * c], fgeo[2 * c + 1]], axis=1).astype(BF16))

    def field_chunk(c):
        g = tile(feat_f[pl.ds(pl.multiple_of(c * 256, 256), 256), :])
        gf[pl.ds(pl.multiple_of(c * 256, 256), 256), :] = g

    early = nz // 4
    each(0, early, field_chunk)

    rs_in[0] = jnp.zeros((WV, SH), BF16)
    total = acc[:, 0:SH]
    each(1, nc, lambda k: arrived(k, rs_in, rs_rs))
    total = total + jnp.sum(rs_in[...].astype(F32), axis=0)
    for k in two_way:
        arrived(k, rsr_in, rsr_rs)
        total = total + rsr_in[k].astype(F32)
    residual = inc[...] - self_term[...] * start - total * scale
    density = start + damping * precondition(residual)
    den_o[...] = density
    den[0] = (density * weight[...]).astype(BF16)
    each(1, nc, lambda k: col_copy(k, den.at[0], den.at[k], den_ss, den_rs).start())

    each(early, nz // 2, field_chunk)
    each(1, nc, lambda k: arrived(k, den, den_rs))
    x = jnp.concatenate([den[k] for k in range(nc)], axis=1)
    fsum = lax.dot_general(x, gf[...], over_lanes, preferred_element_type=F32) * scale
    h, m, l = split3(fsum)
    parts = jnp.concatenate([h.astype(BF16), m.astype(BF16), l.astype(BF16)], axis=0)
    sums = lax.dot_general(parts, onehot[...], over_lanes, preferred_element_type=F32)
    detp[...] = sums[0:WV] + sums[WV:2 * WV] + sums[2 * WV:3 * WV]

    def waves_of(col):
        return pl.ds(pl.multiple_of(lax.rem(col, 2) * 8, 8), 8)

    each(1, nc, lambda k: col_copy(k, detp.at[waves_of(j + k)], det1.at[j], d1_ss, d1_rs).start())
    det1[j] = detp[waves_of(j), :]

    for m in range(nz):
        pot_out[m] = fsum[:, m * 128:(m + 1) * 128].astype(BF16)
    for k, d in enumerate(others):
        row_copy(d, k, pot_out.at[lax.rem(iz + d[0], nz)], pot_in.at[k], pot_ss, pot_rs).start()

    each(1, nc, lambda k: arrived(k, det1, d1_rs))
    det2[iy] = jnp.sum(det1[...], axis=0)
    along_y = [(0, dy) for dy in (ny // 2, *[n for n in range(1, ny) if n != ny // 2])]
    for k, d in enumerate(along_y):
        row_copy(d, k, det2.at[iy], det2.at[iy], d2_ss, d2_rs).start()

    for k in range(ny - 1):
        arrived(k, det2, d2_rs)
    detz[iz] = jnp.sum(det2[...], axis=0)
    for dz in sorted(range(1, nz), key=lambda n: -min(n, nz - n)):
        row_copy((dz, 0), ny - 1 + dz, detz.at[iz], detz.at[iz], d2_ss, d2_rs).start()

    each(0, nr - 1, lambda k: arrived(k, pot_in, pot_rs))
    pot_in[nr - 1] = pot_out[iz]
    pot = jnp.sum(pot_in[...].astype(F32), axis=0)
    pot = pltpu.roll(pot, lax.rem(128 - FD * iy, 128), 1)
    pot_o[...] = pot[:, 0:FD].astype(BF16)

    each(ny, ny + nz - 1, lambda k: arrived(k, detz, d2_rs))
    core = lax.rem(j, 2)
    det3[core] = jnp.sum(detz[...], axis=0) * wave_scale
    swap = pltpu.make_async_remote_copy(
        src_ref=det3.at[core], dst_ref=det3.at[core], send_sem=d3_s.at[0], recv_sem=d3_s.at[1],
        device_id=(i, j + 1 - 2 * core), device_id_type=MESH,
    )
    swap.start()
    swap.wait()
    det_o[...] = jnp.concatenate([det3[0], det3[1]], axis=0)

    def sent(ks, buf, ss):
        def wait(k):
            pltpu.make_async_remote_copy(
                src_ref=buf.at[0], dst_ref=buf.at[0], send_sem=ss.at[k], recv_sem=ss.at[k],
                device_id=(i, j), device_id_type=MESH,
            ).wait_send()

        if isinstance(ks, range):
            each(ks.start, ks.stop, wait)
        else:
            for k in ks:
                wait(k)

    sent(range(1, nc), tgt, tgt_ss)
    sent(range(1, nc), tgx, tgx_ss)
    sent(range(0, own), src, src_ss)
    sent(range(own + 1, len(order)), src, src_ss)
    sent(range(0, nr - 1), fpk, fpk_ss)
    sent(two_way, rsr_out, rsr_ss)
    sent(range(1, nc), rs_out, rs_ss)
    sent(range(1, nc), den, den_ss)
    sent(range(0, nr - 1), pot_out, pot_ss)
    sent(range(1, nc), det1, d1_ss)
    sent(range(0, ny - 1), det2, d2_ss)
    sent(range(ny, ny + nz - 1), detz, d2_ss)


def plan(nz, ny):
    def hops(d):
        return min(d[0], nz - d[0]) + 2 * min(d[1], ny - d[1])

    both = [(dz, dy) for dy in range(1, ny // 2) for dz in range(nz)]
    both += [(dz, dy) for dy in (0, ny // 2) for dz in range(1, nz // 2)]
    both = sorted(both, key=hops)
    pairs = [both[n:n + 2] for n in range(0, len(both), 2)]
    near = pairs[:len(pairs) // 2]
    far = pairs[len(pairs) // 2:][::-1]
    home = [(0, 0), (0, ny // 2)]
    last = [(nz // 2, 0), (nz // 2, ny // 2)]
    seq = near[:1] + [home] + near[1:] + far + [last]
    order = [d for pair in seq for d in pair]
    two_way = [k for k, d in enumerate(order) if d in both]
    return order, two_way, order.index((0, 0))


def local(
    nz, ny, nc, panel_xyz, panel_weight, self_term, panel_slot, block_inverse, incident, field_xyz, field_group
):
    nr = nz * ny
    panels = SH * nr * nc
    fields = field_xyz.shape[1]
    mine = nz * 128
    scale = CYCLES * LEAD / math.sqrt(panels)
    wave_scale = 1.0 / math.sqrt(fields * nr / GROUPS)
    sel_b, sel_a = selectors()
    slots = len(plan(nz, ny)[0])
    vmem, dma = pltpu.VMEM, pltpu.SemaphoreType.DMA
    sems = [dma((10,))]
    for n in (slots, nc, nc, slots, nc, nc, nr, nr, nc, nr):
        sems += [dma((n,)), dma((n,))]
    sems += [dma((2,))]
    args = (
        panel_xyz, panel_weight, self_term.reshape(1, SH), panel_slot.reshape(1, SH), block_inverse, incident,
        field_xyz, field_group.reshape(1, FD), jnp.asarray(sel_b, BF16), jnp.asarray(sel_a, BF16),
    )
    shapes = (
        jax.ShapeDtypeStruct((WV, SH), F32),
        jax.ShapeDtypeStruct((WV, FD), BF16),
        jax.ShapeDtypeStruct((WV, GROUPS), F32),
    )
    hbm = pl.BlockSpec(memory_space=pltpu.HBM)
    results = pl.pallas_call(
        functools.partial(kernel, nz, ny, nc, scale, wave_scale),
        out_shape=shapes,
        in_specs=[pl.BlockSpec(memory_space=pltpu.HBM)] * 10,
        out_specs=(pl.BlockSpec(memory_space=pltpu.VMEM),) * 3,
        scratch_shapes=[vmem(a.shape, a.dtype) for a in args] + [
            vmem((16, SH), F32),
            vmem((2, 8, 128), F32),
            vmem((slots, 32, SH), BF16),
            vmem((nc, 16, SH), BF16),
            vmem((nc, WV, SH), BF16),
            vmem((32, nc * SH), BF16),
            vmem((2 * SH, 32), BF16),
            vmem((mine, 32), BF16),
            vmem((WV, nc * SH), BF16),
            vmem((SH, SH), F32),
            vmem((WV, nc * SH), F32),
            vmem((2 * SH, nc * SH), BF16),
            vmem((slots, WV, SH), BF16),
            vmem((slots, WV, SH), BF16),
            vmem((nc, WV, SH), BF16),
            vmem((nc, WV, SH), BF16),
            vmem((nr, 1, 128), F32),
            vmem((nz, 16, 128), F32),
            vmem((GROUPS, mine), BF16),
            vmem((nc, WV, SH), BF16),
            vmem((mine, nc * SH), BF16),
            vmem((nz, WV, 128), BF16),
            vmem((nr, WV, 128), BF16),
            vmem((WV, GROUPS), F32),
            vmem((nc, 8, GROUPS), F32),
            vmem((ny, 8, GROUPS), F32),
            vmem((nz, 8, GROUPS), F32),
            vmem((2, 8, GROUPS), F32),
        ] + sems,
        compiler_params=pltpu.CompilerParams(
            collective_id=0, has_side_effects=True, vmem_limit_bytes=67043328
        ),
    )(*args)
    return pl.pallas_call(
        hand_out,
        out_shape=shapes,
        in_specs=[hbm] * 3,
        out_specs=(hbm,) * 3,
        scratch_shapes=[vmem(a.shape, a.dtype) for a in shapes] + [dma((3,)), dma((3,))],
        compiler_params=pltpu.CompilerParams(vmem_limit_bytes=67043328),
    )(*results)


def hand_out(a0, a1, a2, o0, o1, o2, s0, s1, s2, in_s, out_s):
    taken = [pltpu.make_async_copy(a, s, in_s.at[n]) for n, (a, s) in enumerate(((a0, s0), (a1, s1), (a2, s2)))]
    given = [pltpu.make_async_copy(s, o, out_s.at[n]) for n, (s, o) in enumerate(((s0, o0), (s1, o1), (s2, o2)))]
    for copy in taken:
        copy.start()
    for copy, put in zip(taken, given):
        copy.wait()
        put.start()
    for put in given:
        put.wait()


def solution(mesh):
    nr, nc = mesh.shape["row"], mesh.shape["col"]
    ny = 4
    return jax.shard_map(
        functools.partial(local, nr // ny, ny, nc),
        mesh=mesh,
        in_specs=(
            P(None, ("col", "row")),
            P(None, ("col", "row")),
            P(("col", "row")),
            P(("col", "row")),
            P(None, ("col", "row")),
            P(None, ("col", "row")),
            P(None, "row"),
            P(("row", "col")),
        ),
        out_specs=(P(None, ("col", "row")), P(None, ("row", "col")), P()),
        check_vma=False,
    )
```

```python
import functools
import math

import jax
import jax.numpy as jnp
import numpy as np
from jax import lax
from jax.experimental import pallas as pl
from jax.experimental.pallas import tpu as pltpu
from jax.sharding import PartitionSpec as P

MESH = pl.DeviceIdType.MESH
HIGHEST = lax.Precision.HIGHEST
F32 = jnp.float32
BF16 = jnp.bfloat16

GROUPS = 128
SH = 128
WV = 16
FD = 32
wave_number = 12.0
smoothing = 0.05
damping = 0.5

LEAD, A1, A0 = 73.90290388562806, -0.5546875, 0.0849609375
CYCLES = wave_number / (2.0 * math.pi)
EPS = smoothing * smoothing * CYCLES * CYCLES


def selectors():
    sel_b = np.zeros((16, 32), np.float32)
    sel_a = np.zeros((32, 16), np.float32)
    high, mid, low = 0, 1, 2
    pairs = [(high, high), (high, mid), (mid, high), (mid, mid), (high, low), (low, high), (mid, low), (low, mid)]
    k = 0
    for b, a in pairs:
        for c in range(3):
            sel_b[3 * b + c, k] = -2.0
            sel_a[k, 3 * a + c] = 1.0
            k += 1
    for n in range(3):
        sel_b[9 + n, k] = 1.0
        sel_a[k, 12] = 1.0
        k += 1
    for n in range(3):
        sel_b[12, k] = 1.0
        sel_a[k, 9 + n] = 1.0
        k += 1
    return sel_b, sel_a


def split3(x):
    h = x.astype(BF16).astype(F32)
    m = (x - h).astype(BF16).astype(F32)
    return h, m, (x - h) - m


def pieces(coords):
    parts = [split3(c) for c in coords]
    norm = split3(coords[0] * coords[0] + coords[1] * coords[1] + coords[2] * coords[2])
    rows = [parts[c][p] for p in range(3) for c in range(3)]
    return rows + list(norm) + [jnp.ones_like(norm[0])]


def pair_values(d):
    s = jnp.maximum(d, 1e-12)
    r = s * lax.rsqrt(s)
    v = (0.25 - jnp.abs(r - jnp.round(r))).astype(BF16)
    q = v * v
    p = (q + BF16(A1)) * q + BF16(A0)
    return (p * v) * lax.rsqrt(s + EPS).astype(BF16)


def kernel(
    nz, ny, nc, scale, wave_scale,
    xyz_h, weight_h, self_h, slot_h, binv_h, inc_h, fxyz_h, fgroup_h, sel_b_h, sel_a_h,
    den_o, pot_o, det_o,
    xyz, weight, self_term, slot, binv, inc, fxyz, fgroup, sel_b, sel_a,
    geo_s, fs, src, tgt, tgx, feat_a, feat_b, feat_f, xt, coupled, acc, gbuf, rsr_out, rsr_in, rs_out, rs_in, fpk, fgeo, onehot,
    den, gf, pot_out, pot_in, detp, det1, det2, det3,
    load_s, src_ss, src_rs, tgt_ss, tgt_rs, tgx_ss, tgx_rs, rsr_ss, rsr_rs, rs_ss, rs_rs, den_ss, den_rs, fpk_ss, fpk_rs,
    pot_ss, pot_rs, d1_ss, d1_rs, d2_ss, d2_rs, d3_s,
):
    nr = nz * ny
    i = lax.axis_index("row")
    j = lax.axis_index("col")
    iz, iy = i // ny, i % ny
    order, two_way, own = plan(nz, ny)
    chunks = len(order) // 2

    def each(lo, hi, body):
        def step(n, _):
            body(n)
            return 0

        lax.fori_loop(lo, hi, step, 0)

    barrier = pltpu.get_barrier_semaphore()
    each(0, nr - 1, lambda n: pl.semaphore_signal(
        barrier, inc=1, device_id=(lax.rem(i + 1 + lax.rem(n + nr // 2 - 1, nr - 1), nr), j), device_id_type=MESH))
    each(1, nc, lambda n: pl.semaphore_signal(
        barrier, inc=1, device_id=(i, lax.rem(j + n, nc)), device_id_type=MESH))

    loads = [
        pltpu.make_async_copy(a, b, load_s.at[n])
        for n, (a, b) in enumerate([
            (xyz_h, xyz), (weight_h, weight), (self_h, self_term), (slot_h, slot), (binv_h, binv), (inc_h, inc),
            (fxyz_h, fxyz), (fgroup_h, fgroup), (sel_b_h, sel_b), (sel_a_h, sel_a),
        ])
    ]
    for load in loads:
        load.start()
    for load in loads:
        load.wait()

    rows = pieces([xyz[c:c + 1, :] * CYCLES for c in range(3)])
    for n, row in enumerate(rows):
        geo_s[n:n + 1, :] = row
    geo_s[13:16, :] = jnp.zeros((3, SH), F32)
    packet = geo_s[...].astype(BF16)
    src[own, 0:16, :] = packet
    tgt[0] = packet
    place = lax.broadcasted_iota(jnp.int32, (64, SH), 0)
    chosen = (place == slot[...] % 64).astype(F32)
    half = (lax.broadcasted_iota(jnp.int32, (8, SH), 0) == slot[...] // 64).astype(F32)
    over_rows = (((0,), (0,)), ((), ()))
    over_lanes = (((1,), (1,)), ((), ()))
    picked = lax.dot_general(binv[...], chosen, over_rows, precision=HIGHEST, preferred_element_type=F32)
    same = lax.dot_general(half, half, over_rows, preferred_element_type=F32)
    coupled[...] = picked * same

    def precondition(values):
        mixing = jnp.dot(values, coupled[...], precision=HIGHEST, preferred_element_type=F32)
        return values / self_term[...] + mixing

    start = precondition(inc[...])
    start_w = (start * weight[...]).astype(BF16)
    src[own, 16:32, :] = start_w
    tgx[0] = start_w

    lane = lax.broadcasted_iota(jnp.int32, (8, 128), 1)
    fs[...] = jnp.zeros_like(fs)
    fs[0, 0:3, :] = fxyz[:, pl.ds(pl.multiple_of(j // 4 * 128, 128), 128)]
    fs[1, 0:1, 0:FD] = fgroup[...].astype(F32)
    points = pltpu.roll(fs[0], lax.rem(128 - FD * lax.rem(j, 4), 128), 1)
    points = jnp.where(lane < FD, points, 0.0)
    row = points[0:1] + pltpu.roll(points, FD, 1)[1:2] + pltpu.roll(points, 2 * FD, 1)[2:3]
    row = row + pltpu.roll(fs[1], 3 * FD, 1)[0:1]
    mine = iy * nz + iz
    fpk[mine] = row

    pl.semaphore_wait(barrier, nr + nc - 2)

    def row_copy(d, k, src_ref, dst_ref, ss, rs):
        dz, dy = d
        peer = lax.rem(iz + dz % nz, nz) * ny + lax.rem(iy + dy % ny, ny)
        return pltpu.make_async_remote_copy(
            src_ref=src_ref, dst_ref=dst_ref, send_sem=ss.at[k], recv_sem=rs.at[k],
            device_id=(peer, j), device_id_type=MESH,
        )

    def col_copy(k, src_ref, dst_ref, ss, rs):
        return pltpu.make_async_remote_copy(
            src_ref=src_ref, dst_ref=dst_ref, send_sem=ss.at[k], recv_sem=rs.at[k],
            device_id=(i, lax.rem(j + k, nc)), device_id_type=MESH,
        )

    def arrived(k, buf, rs):
        pltpu.make_async_remote_copy(
            src_ref=buf.at[0], dst_ref=buf.at[0], send_sem=rs.at[k], recv_sem=rs.at[k],
            device_id=(i, j), device_id_type=MESH,
        ).wait_recv()

    each(1, nc, lambda k: col_copy(k, tgt.at[0], tgt.at[k], tgt_ss, tgt_rs).start())
    for k, (dz, dy) in enumerate(order):
        if k == 4:
            each(1, nc, lambda n: col_copy(n, tgx.at[0], tgx.at[n], tgx_ss, tgx_rs).start())
        if k != own:
            row_copy((-dz, -dy), k, src.at[own], src.at[k], src_ss, src_rs).start()
    others = sorted([(dz, dy) for dz in range(nz) for dy in range(ny)][1:],
                    key=lambda d: -min(d[0], nz - d[0]) - 2 * min(d[1], ny - d[1]))
    for k, d in enumerate(others):
        row_copy(d, k, fpk.at[mine], fpk.at[mine], fpk_ss, fpk_rs).start()

    def features_a(pk):
        return jnp.dot(sel_a[...], pk, preferred_element_type=F32).astype(BF16)

    def features_b(pk):
        return lax.dot_general(pk, sel_b[...], over_rows, preferred_element_type=F32).astype(BF16)

    acc[...] = jnp.zeros_like(acc)

    def tile(b):
        return pair_values(jnp.dot(b, feat_a[...], preferred_element_type=F32))

    def source_features(c):
        return features_b(jnp.concatenate([src[2 * c, 0:16, :], src[2 * c + 1, 0:16, :]], axis=1))

    def use(c, last=False):
        x = jnp.concatenate([src[2 * c, 16:32, :], src[2 * c + 1, 16:32, :]], axis=1)
        g = gbuf[...]
        acc[...] += jnp.dot(x, g, preferred_element_type=F32)
        if last:
            return
        back = lax.dot_general(xt[...], g, over_lanes, preferred_element_type=F32).astype(BF16)
        rsr_out[2 * c] = back[:, 0:SH]
        rsr_out[2 * c + 1] = back[:, SH:2 * SH]

    def wait_chunk(c):
        @pl.when(c != own // 2)
        def _():
            arrived(2 * c, src, src_rs)

        arrived(2 * c + 1, src, src_rs)

    def images_chunk(c):
        @pl.when(c + 1 < chunks)
        def _():
            wait_chunk(c + 1)

        b = feat_b[...]
        use(c - 1)
        gbuf[...] = tile(b)
        feat_b[...] = source_features(jnp.minimum(c + 1, chunks - 1))
        for k in two_way:
            @pl.when(c - 1 == k // 2)
            def _():
                row_copy(order[k], k, rsr_out.at[k], rsr_in.at[k], rsr_ss, rsr_rs).start()

    wait_chunk(0)
    first = source_features(0)
    wait_chunk(1)
    feat_b[...] = source_features(1)
    each(1, nc, lambda k: arrived(k, tgt, tgt_rs))
    for k in range(0, nc, 4):
        feat_a[:, k * SH:(k + 4) * SH] = features_a(jnp.concatenate([tgt[n] for n in range(k, k + 4)], axis=1))
    gbuf[...] = tile(first)
    each(1, nc, lambda k: arrived(k, tgx, tgx_rs))
    for k in range(nc):
        xt[:, k * SH:(k + 1) * SH] = tgx[k]
    each(1, chunks, images_chunk)
    use(chunks - 1, last=True)

    def rs_send(k):
        rs_out[k] = acc[:, pl.ds(pl.multiple_of(k * SH, SH), SH)].astype(BF16)
        pltpu.make_async_remote_copy(
            src_ref=rs_out.at[k], dst_ref=rs_in.at[k], send_sem=rs_ss.at[k], recv_sem=rs_rs.at[k],
            device_id=(i, lax.rem(j + nc - k, nc)), device_id_type=MESH,
        ).start()

    each(1, nc, rs_send)

    each(0, nr - 1, lambda k: arrived(k, fpk, fpk_rs))
    packets = fpk[...].reshape(nr, 128)
    quarter = lax.broadcasted_iota(jnp.int32, (nz, 128), 1) // FD
    comps = []
    for c in range(4):
        comp = jnp.zeros((nz, 128), F32)
        for a in range(ny):
            moved = packets[a * nz:(a + 1) * nz]
            if a != c:
                moved = pltpu.roll(moved, FD * (a - c) % 128, 1)
            comp = jnp.where(quarter == a, moved, comp)
        comps.append(comp)
    frows = pieces([comp * CYCLES for comp in comps[:3]])
    detectors = lax.broadcasted_iota(jnp.int32, (GROUPS, 128), 0).astype(F32)
    for m in range(nz):
        for n, part in enumerate(frows):
            fgeo[m, n:n + 1, :] = part[m:m + 1]
        fgeo[m, 13:16, :] = jnp.zeros((3, 128), F32)
        onehot[:, m * 128:(m + 1) * 128] = (detectors == comps[3][m:m + 1]).astype(BF16)

    for c in range(nz // 2):
        feat_f[c * 256:(c + 1) * 256, :] = features_b(
            jnp.concatenate([fgeo[2 * c], fgeo[2 * c + 1]], axis=1).astype(BF16))

    def field_chunk(c):
        g = tile(feat_f[pl.ds(pl.multiple_of(c * 256, 256), 256), :])
        gf[pl.ds(pl.multiple_of(c * 256, 256), 256), :] = g

    early = nz // 4
    each(0, early, field_chunk)

    rs_in[0] = jnp.zeros((WV, SH), BF16)
    total = acc[:, 0:SH]
    each(1, nc, lambda k: arrived(k, rs_in, rs_rs))
    total = total + jnp.sum(rs_in[...].astype(F32), axis=0)
    for k in two_way:
        arrived(k, rsr_in, rsr_rs)
        total = total + rsr_in[k].astype(F32)
    residual = inc[...] - self_term[...] * start - total * scale
    density = start + damping * precondition(residual)
    den_o[...] = density
    den[0] = (density * weight[...]).astype(BF16)
    each(1, nc, lambda k: col_copy(k, den.at[0], den.at[k], den_ss, den_rs).start())

    each(early, nz // 2, field_chunk)
    each(1, nc, lambda k: arrived(k, den, den_rs))
    x = jnp.concatenate([den[k] for k in range(nc)], axis=1)
    fsum = lax.dot_general(x, gf[...], over_lanes, preferred_element_type=F32) * scale
    h, m, l = split3(fsum)
    parts = jnp.concatenate([h.astype(BF16), m.astype(BF16), l.astype(BF16)], axis=0)
    sums = lax.dot_general(parts, onehot[...], over_lanes, preferred_element_type=F32)
    detp[...] = sums[0:WV] + sums[WV:2 * WV] + sums[2 * WV:3 * WV]

    def waves_of(col):
        return pl.ds(pl.multiple_of(lax.rem(col, 2) * 8, 8), 8)

    each(1, nc, lambda k: col_copy(k, detp.at[waves_of(j + k)], det1.at[j], d1_ss, d1_rs).start())
    det1[j] = detp[waves_of(j), :]

    for m in range(nz):
        pot_out[m] = fsum[:, m * 128:(m + 1) * 128].astype(BF16)
    for k, d in enumerate(others):
        row_copy(d, k, pot_out.at[lax.rem(iz + d[0], nz)], pot_in.at[k], pot_ss, pot_rs).start()

    each(1, nc, lambda k: arrived(k, det1, d1_rs))
    det2[i] = jnp.sum(det1[...], axis=0)
    for k, d in enumerate(others):
        row_copy(d, k, det2.at[i], det2.at[i], d2_ss, d2_rs).start()

    each(0, nr - 1, lambda k: arrived(k, pot_in, pot_rs))
    pot_in[nr - 1] = pot_out[iz]
    pot = jnp.sum(pot_in[...].astype(F32), axis=0)
    pot = pltpu.roll(pot, lax.rem(128 - FD * iy, 128), 1)
    pot_o[...] = pot[:, 0:FD].astype(BF16)

    each(0, nr - 1, lambda k: arrived(k, det2, d2_rs))
    core = lax.rem(j, 2)
    det3[core] = jnp.sum(det2[...], axis=0) * wave_scale
    swap = pltpu.make_async_remote_copy(
        src_ref=det3.at[core], dst_ref=det3.at[core], send_sem=d3_s.at[0], recv_sem=d3_s.at[1],
        device_id=(i, j + 1 - 2 * core), device_id_type=MESH,
    )
    swap.start()
    swap.wait()
    det_o[...] = jnp.concatenate([det3[0], det3[1]], axis=0)

    def sent(ks, buf, ss):
        def wait(k):
            pltpu.make_async_remote_copy(
                src_ref=buf.at[0], dst_ref=buf.at[0], send_sem=ss.at[k], recv_sem=ss.at[k],
                device_id=(i, j), device_id_type=MESH,
            ).wait_send()

        if isinstance(ks, range):
            each(ks.start, ks.stop, wait)
        else:
            for k in ks:
                wait(k)

    sent(range(1, nc), tgt, tgt_ss)
    sent(range(1, nc), tgx, tgx_ss)
    sent(range(0, own), src, src_ss)
    sent(range(own + 1, len(order)), src, src_ss)
    sent(range(0, nr - 1), fpk, fpk_ss)
    sent(two_way, rsr_out, rsr_ss)
    sent(range(1, nc), rs_out, rs_ss)
    sent(range(1, nc), den, den_ss)
    sent(range(0, nr - 1), pot_out, pot_ss)
    sent(range(1, nc), det1, d1_ss)
    sent(range(0, nr - 1), det2, d2_ss)


def plan(nz, ny):
    def hops(d):
        return min(d[0], nz - d[0]) + 2 * min(d[1], ny - d[1])

    both = [(dz, dy) for dy in range(1, ny // 2) for dz in range(nz)]
    both += [(dz, dy) for dy in (0, ny // 2) for dz in range(1, nz // 2)]
    both = sorted(both, key=hops)
    pairs = [both[n:n + 2] for n in range(0, len(both), 2)]
    near = pairs[:len(pairs) // 2]
    far = pairs[len(pairs) // 2:][::-1]
    home = [(0, 0), (0, ny // 2)]
    last = [(nz // 2, 0), (nz // 2, ny // 2)]
    seq = near[:1] + [home] + near[1:] + far + [last]
    order = [d for pair in seq for d in pair]
    two_way = [k for k, d in enumerate(order) if d in both]
    return order, two_way, order.index((0, 0))


def local(
    nz, ny, nc, panel_xyz, panel_weight, self_term, panel_slot, block_inverse, incident, field_xyz, field_group
):
    nr = nz * ny
    panels = SH * nr * nc
    fields = field_xyz.shape[1]
    mine = nz * 128
    scale = CYCLES * LEAD / math.sqrt(panels)
    wave_scale = 1.0 / math.sqrt(fields * nr / GROUPS)
    sel_b, sel_a = selectors()
    slots = len(plan(nz, ny)[0])
    vmem, dma = pltpu.VMEM, pltpu.SemaphoreType.DMA
    sems = [dma((10,))]
    for n in (slots, nc, nc, slots, nc, nc, nr, nr, nc, nr):
        sems += [dma((n,)), dma((n,))]
    sems += [dma((2,))]
    args = (
        panel_xyz, panel_weight, self_term.reshape(1, SH), panel_slot.reshape(1, SH), block_inverse, incident,
        field_xyz, field_group.reshape(1, FD), jnp.asarray(sel_b, BF16), jnp.asarray(sel_a, BF16),
    )
    shapes = (
        jax.ShapeDtypeStruct((WV, SH), F32),
        jax.ShapeDtypeStruct((WV, FD), BF16),
        jax.ShapeDtypeStruct((WV, GROUPS), F32),
    )
    hbm = pl.BlockSpec(memory_space=pltpu.HBM)
    results = pl.pallas_call(
        functools.partial(kernel, nz, ny, nc, scale, wave_scale),
        out_shape=shapes,
        in_specs=[pl.BlockSpec(memory_space=pltpu.HBM)] * 10,
        out_specs=(pl.BlockSpec(memory_space=pltpu.VMEM),) * 3,
        scratch_shapes=[vmem(a.shape, a.dtype) for a in args] + [
            vmem((16, SH), F32),
            vmem((2, 8, 128), F32),
            vmem((slots, 32, SH), BF16),
            vmem((nc, 16, SH), BF16),
            vmem((nc, WV, SH), BF16),
            vmem((32, nc * SH), BF16),
            vmem((2 * SH, 32), BF16),
            vmem((mine, 32), BF16),
            vmem((WV, nc * SH), BF16),
            vmem((SH, SH), F32),
            vmem((WV, nc * SH), F32),
            vmem((2 * SH, nc * SH), BF16),
            vmem((slots, WV, SH), BF16),
            vmem((slots, WV, SH), BF16),
            vmem((nc, WV, SH), BF16),
            vmem((nc, WV, SH), BF16),
            vmem((nr, 1, 128), F32),
            vmem((nz, 16, 128), F32),
            vmem((GROUPS, mine), BF16),
            vmem((nc, WV, SH), BF16),
            vmem((mine, nc * SH), BF16),
            vmem((nz, WV, 128), BF16),
            vmem((nr, WV, 128), BF16),
            vmem((WV, GROUPS), F32),
            vmem((nc, 8, GROUPS), F32),
            vmem((nr, 8, GROUPS), F32),
            vmem((2, 8, GROUPS), F32),
        ] + sems,
        compiler_params=pltpu.CompilerParams(
            collective_id=0, has_side_effects=True, vmem_limit_bytes=67043328
        ),
    )(*args)
    return pl.pallas_call(
        hand_out,
        out_shape=shapes,
        in_specs=[hbm] * 3,
        out_specs=(hbm,) * 3,
        scratch_shapes=[vmem(a.shape, a.dtype) for a in shapes] + [dma((3,)), dma((3,))],
        compiler_params=pltpu.CompilerParams(vmem_limit_bytes=67043328),
    )(*results)


def hand_out(a0, a1, a2, o0, o1, o2, s0, s1, s2, in_s, out_s):
    taken = [pltpu.make_async_copy(a, s, in_s.at[n]) for n, (a, s) in enumerate(((a0, s0), (a1, s1), (a2, s2)))]
    given = [pltpu.make_async_copy(s, o, out_s.at[n]) for n, (s, o) in enumerate(((s0, o0), (s1, o1), (s2, o2)))]
    for copy in taken:
        copy.start()
    for copy, put in zip(taken, given):
        copy.wait()
        put.start()
    for put in given:
        put.wait()


def solution(mesh):
    nr, nc = mesh.shape["row"], mesh.shape["col"]
    ny = 4
    return jax.shard_map(
        functools.partial(local, nr // ny, ny, nc),
        mesh=mesh,
        in_specs=(
            P(None, ("col", "row")),
            P(None, ("col", "row")),
            P(("col", "row")),
            P(("col", "row")),
            P(None, ("col", "row")),
            P(None, ("col", "row")),
            P(None, "row"),
            P(("row", "col")),
        ),
        out_specs=(P(None, ("col", "row")), P(None, ("row", "col")), P()),
        check_vma=False,
    )
```
